32 devices in a mesh: gx: 4 (over z), gy: 8 (over y, x, core).
Axes of the slice: x: 2, y: 2, z: 4, core: 2. Of those that a mesh axis runs over, the one named last changes fastest.
Arguments:
- orders: int32 [4, 8, 128], P('gx', 'gy'), may hold values from 3 to 7
- velocity: bfloat16 [4, 8, 3, 512, 128], P('gx', 'gy'), may hold values from -0.29882812 to 0.29882812
- adjoint_field: float32 [4, 8, 3, 512, 128], P('gx', 'gy'), may hold values from -0.3 to 0.3
- face_links: int32 [4, 8, 6, 128], P('gx', 'gy'), may hold values from 0 to 1280, as said below
- orient: int32 [4, 8, 6, 128], P('gx', 'gy'), may hold values from 0 to 3, as said below
- send_faces: int32 [4, 8, 4, 128], P('gx', 'gy'), may hold values from 0 to 768, as said below
Outputs:
- adjoint_image: float32 [4, 8, 3, 512, 128], P('gx', 'gy')
The draws below stay inside these ranges and needn't reach their ends.
Inputs may be any that keep to these rules, and one draw needn't show every extreme that they name: `face_links`: own face ids, received slots 6 * 128 + k * 128 + s, or the wall column 1280; links are mutual, a face never links to a received slot that its neighbour leaves empty, and faces toward a missing neighbour are walls. `orient`: both sides of a face carry the same orientation. `send_faces`: each own face appears at most once; 768 marks an empty slot; some neighbour pair fills all 128 slots.
All inputs are finite; a program needn't handle non-finite values.
Results may differ from the reference program's by a relative error of at most 0.0003.
Values sent between devices are 32-bit elements; how exact they have to be, the bound alone decides.
No kernel may reach another device: no remote copies, remote signals or barrier semaphores. Data moves between devices by JAX's collectives and lax.ppermute only.
A program may use at most 64 MiB of HBM per device.

```python
import math
import jax
import jax.numpy as jnp
from jax import lax

MODES = 512
E_DEV = 128
F_DIR = 128
N_GX = 4
N_GY = 8


def face_graph(key):
    face_slots = 6 * E_DEV
    band_end = 4 * F_DIR
    least = F_DIR // 2
    counts_x = jax.random.randint(jax.random.fold_in(key, 1), (N_GX - 1, N_GY), least, F_DIR + 1).at[0, 0].set(F_DIR)
    counts_y = jax.random.randint(jax.random.fold_in(key, 2), (N_GX, N_GY - 1), least, F_DIR + 1).at[0, 0].set(F_DIR)
    turn_x = jax.random.randint(jax.random.fold_in(key, 3), (N_GX - 1, N_GY, F_DIR), 0, 4)
    turn_y = jax.random.randint(jax.random.fold_in(key, 4), (N_GX, N_GY - 1, F_DIR), 0, 4)
    counts = jnp.stack([jnp.pad(counts_x, ((0, 1), (0, 0))), jnp.pad(counts_x, ((1, 0), (0, 0))), jnp.pad(counts_y, ((0, 0), (0, 1))), jnp.pad(counts_y, ((0, 0), (1, 0)))], axis=-1)
    turns = jnp.stack([jnp.pad(turn_x, ((0, 1), (0, 0), (0, 0))), jnp.pad(turn_x, ((1, 0), (0, 0), (0, 0))), jnp.pad(turn_y, ((0, 0), (0, 1), (0, 0))), jnp.pad(turn_y, ((0, 0), (1, 0), (0, 0)))], axis=2)
    device_keys = jax.random.split(jax.random.fold_in(key, 5), N_GX * N_GY)
    order_of = jax.vmap(lambda k: jax.random.permutation(k, face_slots))(device_keys).reshape(N_GX, N_GY, face_slots).astype(jnp.int32)
    placed = jnp.argsort(order_of, axis=-1, stable=True).astype(jnp.int32)
    position = jnp.arange(face_slots, dtype=jnp.int32)
    direction = jnp.minimum(position // F_DIR, 3)
    within = position % F_DIR
    live_count = counts[:, :, direction]
    banded = position < band_end
    used = banded & (within < live_count)
    partner_pos = band_end + jnp.bitwise_xor(jnp.maximum(position - band_end, 0), 1)
    partner_pos = jnp.where(banded, position, partner_pos)
    shape = order_of.shape
    partner_face = jnp.take_along_axis(order_of, jnp.broadcast_to(partner_pos, shape), axis=-1)
    link_pos = jnp.where(used, face_slots + direction * F_DIR + within, jnp.where(banded, face_slots + band_end, partner_face))
    pair_turn = jax.random.randint(jax.random.fold_in(key, 6), shape, 0, 4)
    pair_first = jnp.where(banded, position, band_end + jnp.maximum(position - band_end, 0) // 2 * 2)
    pair_turn_pos = jnp.take_along_axis(pair_turn, jnp.broadcast_to(pair_first, shape), axis=-1)
    flat_turns = turns.reshape(N_GX, N_GY, band_end)
    iface_turn = jnp.take_along_axis(flat_turns, jnp.broadcast_to(jnp.minimum(position, band_end - 1), shape), axis=-1)
    turn_pos = jnp.where(banded, iface_turn, pair_turn_pos)
    face_links = jnp.take_along_axis(link_pos, placed, axis=-1).reshape(N_GX, N_GY, 6, E_DEV)
    orient = jnp.take_along_axis(turn_pos, placed, axis=-1).reshape(N_GX, N_GY, 6, E_DEV)
    slot_index = jnp.arange(F_DIR, dtype=jnp.int32)
    heads = order_of[:, :, :band_end].reshape(N_GX, N_GY, 4, F_DIR)
    send_faces = jnp.where(slot_index[None, None, None, :] < counts[:, :, :, None], heads, face_slots)
    return (face_links.astype(jnp.int32), orient.astype(jnp.int32), send_faces.astype(jnp.int32))


def draw_face_links(key, part):
    return face_graph(key)[0]


def draw_orient(key, part):
    return face_graph(key)[1]


def draw_send_faces(key, part):
    return face_graph(key)[2]


def set_ends(values, key, low, high):
    index_at = [jax.random.randint(jax.random.fold_in(key, axis), (), 0, length) for axis, length in enumerate(values.shape)]
    widest = values.shape.index(max(values.shape))
    neighbour = index_at[:widest] + [(index_at[widest] + 1) % values.shape[widest]] + index_at[widest + 1:]
    return values.at[tuple(index_at)].set(low).at[tuple(neighbour)].set(high)


def levels(stream_key, shape, shards, low, largest):
    def one(axis_at, blocks):
        draws = jax.random.uniform(jax.random.fold_in(jax.random.fold_in(stream_key, 6), axis_at), (blocks,), jnp.float32, low / len(shards), largest / len(shards))
        return jnp.repeat(jnp.exp(draws), shape[axis_at] // blocks).reshape((-1,) + (1,) * (len(shape) - axis_at - 1))

    loudness = one(*shards[0])
    for cut in shards[1:]:
        loudness = loudness * one(*cut)
    return loudness


def bell_draw(stream_key, shape, deviation, limit, shards=(), kind=jnp.bfloat16):
    values = jax.random.normal(stream_key, shape, jnp.float32) * deviation
    if len(shards) > 0:
        values = levels(stream_key, shape, shards, -0.22, 0.18) * values
    return jnp.clip(values, min=-limit, max=limit).astype(kind)


def setup_inputs(seed: int = 0) -> dict:
    key_of = jax.random.split(jax.random.key(seed), 7)
    return {
        "orders": set_ends(jax.random.randint(key_of[0], (N_GX, N_GY, E_DEV), 3, 8), jax.random.fold_in(key_of[0], 1), 3, 7).astype(jnp.int32),
        "velocity": bell_draw(key_of[1], (N_GX, N_GY, 3, MODES, E_DEV), 0.05, 0.29882812, ((0, 4), (1, 8))),
        "adjoint_field": bell_draw(key_of[2], (N_GX, N_GY, 3, MODES, E_DEV), 0.05, 0.3, ((0, 4), (1, 8)), jnp.float32),
        "face_links": draw_face_links(jax.random.fold_in(key_of[6], 71), 0),
        "orient": draw_orient(jax.random.fold_in(key_of[6], 71), 0),
        "send_faces": draw_send_faces(jax.random.fold_in(key_of[6], 71), 0),
    }


ETA = 1.0
YIELD = 2.0
DELTA = 0.05
PENALTY = 2.0
HIGHEST = lax.Precision.HIGHEST

def basis_tables():
    mode_index = jnp.arange(8, dtype=jnp.float32)
    points = jnp.cos(math.pi * (mode_index + 0.5) / 8.0)
    weights = math.pi / 8.0 * jnp.sqrt(1.0 - points * points)
    values = [jnp.ones_like(points), points]
    slopes = [jnp.zeros_like(points), jnp.ones_like(points)]
    for k in range(1, 7):
        values.append(((2 * k + 1) * points * values[k] - k * values[k - 1]) / (k + 1))
        slopes.append(slopes[k - 1] + (2 * k + 1) * values[k])
    legendre = jnp.stack(values, axis=1)
    legendre_slope = jnp.stack(slopes, axis=1)
    parity = jnp.where(jnp.arange(8) % 2 == 0, 1.0, -1.0).astype(jnp.float32)
    slope_end = mode_index * (mode_index + 1.0) / 2.0
    ends_value = jnp.stack([parity, jnp.ones(8, jnp.float32)])
    ends_slope = jnp.stack([parity * slope_end, slope_end])
    face_mass = 2.0 / (2.0 * mode_index + 1.0)
    return (legendre, legendre_slope, weights, ends_value, ends_slope, face_mass)

def apply_along(matrix, coef, axis):
    patterns = ['', 'qi,cijke->cqjke', 'qj,cijke->ciqke', 'qk,cijke->cijqe']
    return jnp.einsum(patterns[axis], matrix, coef, precision=HIGHEST)

def point_gradient(coef, legendre, legendre_slope):
    inner_k = apply_along(legendre, coef, 3)
    inner_jk = apply_along(legendre, inner_k, 2)
    grad_x = apply_along(legendre_slope, inner_jk, 1)
    grad_y = apply_along(legendre, apply_along(legendre_slope, inner_k, 2), 1)
    grad_z = apply_along(legendre, apply_along(legendre, apply_along(legendre_slope, coef, 3), 2), 1)
    return jnp.stack([grad_x, grad_y, grad_z])

def point_divergence(stress, legendre, legendre_slope):
    plain_t = legendre.T
    slope_t = legendre_slope.T
    part_x = apply_along(plain_t, apply_along(plain_t, apply_along(slope_t, stress[0], 1), 2), 3)
    part_y = apply_along(plain_t, apply_along(slope_t, apply_along(plain_t, stress[1], 1), 2), 3)
    part_z = apply_along(slope_t, apply_along(plain_t, apply_along(plain_t, stress[2], 1), 2), 3)
    return part_x + part_y + part_z

def live_mask(order_dev):
    mode_index = jnp.arange(8, dtype=jnp.int32)
    alive = (mode_index[:, None] <= order_dev[None, :]).astype(jnp.float32)
    return alive[:, None, None, :] * alive[None, :, None, :] * alive[None, None, :, :]

def prepare(order_dev, velocity_dev, field_dev):
    elements = order_dev.shape[0]
    live_modes = live_mask(order_dev)
    coef_u = velocity_dev.astype(jnp.float32).reshape(3, 8, 8, 8, elements) * live_modes
    coef_v = field_dev.astype(jnp.float32).reshape(3, 8, 8, 8, elements) * live_modes
    return (live_modes, coef_u, coef_v)

def cube_weights(weights):
    return (weights[:, None, None] * weights[None, :, None] * weights[None, None, :])[:, :, :, None]

def state_terms(coef_u, tables_all):
    legendre, legendre_slope, weights = (tables_all[0], tables_all[1], tables_all[2])
    grad_u = point_gradient(coef_u, legendre, legendre_slope)
    strain_u = 0.5 * (grad_u + jnp.swapaxes(grad_u, 0, 1))
    rate_sq = 2.0 * lax.optimization_barrier(jnp.sum(strain_u * strain_u, axis=(0, 1)))
    regular = jnp.sqrt(rate_sq + DELTA * DELTA)
    viscosity = ETA + YIELD / regular
    cube_weight = cube_weights(weights)
    mean_visc = lax.optimization_barrier(jnp.sum(cube_weight * viscosity, axis=(0, 1, 2))) / jnp.sum(cube_weight)
    return (strain_u, regular, viscosity, mean_visc)

def volume_terms(coef_v, strain_u, regular, viscosity, tables_all):
    legendre, legendre_slope, weights = (tables_all[0], tables_all[1], tables_all[2])
    grad_v = point_gradient(coef_v, legendre, legendre_slope)
    strain_v = 0.5 * (grad_v + jnp.swapaxes(grad_v, 0, 1))
    contract = lax.optimization_barrier(jnp.sum(strain_u * strain_v, axis=(0, 1)))
    cube_weight = cube_weights(weights)
    stress = cube_weight * (2.0 * viscosity * strain_v - 4.0 * YIELD * contract / (regular * regular * regular) * strain_u)
    return point_divergence(stress, legendre, legendre_slope)

def face_trace(coef, ends, face_id):
    patterns = ['i,cijke->cjke', 'j,cijke->cike', 'k,cijke->cije']
    return jnp.einsum(patterns[face_id // 2], ends[face_id % 2], coef, precision=HIGHEST)

def face_lift(trace, ends, face_id):
    patterns = ['i,cjke->cijke', 'j,cike->cijke', 'k,cije->cijke']
    return jnp.einsum(patterns[face_id // 2], ends[face_id % 2], trace, precision=HIGHEST)

def face_tables(coef_v, tables_all):
    ends_value, ends_slope = (tables_all[3], tables_all[4])
    elements = coef_v.shape[-1]
    local_value = jnp.concatenate([face_trace(coef_v, ends_value, f).reshape(192, elements) for f in range(6)], axis=1)
    local_slope = jnp.concatenate([face_trace(coef_v, ends_slope, f).reshape(192, elements) for f in range(6)], axis=1)
    return (local_value, local_slope)

def face_terms(local_value, local_slope, mean_visc, order_dev, face_links, orient, recv_value, recv_flux, recv_visc, recv_order, tables_all):
    ends_value, ends_slope, face_mass = (tables_all[3], tables_all[4], tables_all[5])
    elements = order_dev.shape[0]
    face_slots = 6 * elements
    face_visc = jnp.tile(mean_visc, 6)
    face_order = jnp.tile(order_dev, 6)
    local_flux = local_slope * face_visc[None, :]
    zero_column = jnp.zeros((192, 1), jnp.float32)
    value_all = jnp.concatenate([local_value, recv_value, zero_column], axis=1)
    flux_all = jnp.concatenate([local_flux, recv_flux, zero_column], axis=1)
    visc_all = jnp.concatenate([face_visc, recv_visc, jnp.zeros((1,), jnp.float32)])
    order_all = jnp.concatenate([face_order, recv_order, jnp.zeros((1,), jnp.int32)])
    target = face_links.reshape(-1)
    orient_flat = orient.reshape(-1)
    far_value = jnp.take(value_all, target, axis=1).reshape(3, 8, 8, face_slots)
    far_flux = jnp.take(flux_all, target, axis=1).reshape(3, 8, 8, face_slots)
    far_visc = jnp.take(visc_all, target)
    far_order = jnp.take(order_all, target)
    parity = ends_value[0]
    flip_first = jnp.where((orient_flat % 2)[None, :] == 1, parity[:, None], 1.0)
    flip_second = jnp.where((orient_flat // 2)[None, :] == 1, parity[:, None], 1.0)
    rotation = flip_first[:, None, :] * flip_second[None, :, :]
    jumps = local_value.reshape(3, 8, 8, face_slots) - rotation * far_value
    at_wall = target == face_slots + recv_value.shape[1]
    weight_half = jnp.where(at_wall, 1.0, 0.5).astype(jnp.float32)
    highest = (jnp.maximum(face_order, far_order) + 1).astype(jnp.float32)
    penalty = PENALTY * highest * highest * jnp.maximum(face_visc, far_visc)
    face_weight = (face_mass[:, None] * face_mass[None, :])[:, :, None]
    own_flux = local_flux.reshape(3, 8, 8, face_slots)
    value_part = face_weight * (penalty * jumps - weight_half * own_flux + weight_half * rotation * far_flux)
    slope_part = face_weight * (-weight_half * face_visc * jumps)
    lifted = jnp.zeros((3, 8, 8, 8, elements), jnp.float32)
    for face_id in range(6):
        window = slice(face_id * elements, (face_id + 1) * elements)
        lifted = lifted + face_lift(value_part[..., window], ends_value, face_id)
        lifted = lifted + face_lift(slope_part[..., window], ends_slope, face_id)
    return lifted

def outgoing(order_dev, velocity_dev, field_dev, send_dev, tables_all):
    live_modes, coef_u, coef_v = prepare(order_dev, velocity_dev, field_dev)
    strain_u, regular, viscosity, mean_visc = state_terms(coef_u, tables_all)
    local_value, local_slope = face_tables(coef_v, tables_all)
    zero_column = jnp.zeros((192, 1), jnp.float32)
    face_visc = jnp.concatenate([jnp.tile(mean_visc, 6), jnp.zeros((1,), jnp.float32)])
    face_order = jnp.concatenate([jnp.tile(order_dev, 6), jnp.zeros((1,), jnp.int32)])
    padded_value = jnp.concatenate([local_value, zero_column], axis=1)
    padded_flux = jnp.concatenate([local_slope, zero_column], axis=1) * face_visc[None, :]
    value_out = jnp.moveaxis(jnp.take(padded_value, send_dev, axis=1), 1, 0)
    flux_out = jnp.moveaxis(jnp.take(padded_flux, send_dev, axis=1), 1, 0)
    return (value_out, flux_out, jnp.take(face_visc, send_dev), jnp.take(face_order, send_dev))

def neighbour_view(packet):
    from_up_x = jnp.concatenate([packet[1:, :, 1], jnp.zeros_like(packet[:1, :, 1])], axis=0)
    from_down_x = jnp.concatenate([jnp.zeros_like(packet[:1, :, 0]), packet[:-1, :, 0]], axis=0)
    from_up_y = jnp.concatenate([packet[:, 1:, 3], jnp.zeros_like(packet[:, :1, 3])], axis=1)
    from_down_y = jnp.concatenate([jnp.zeros_like(packet[:, :1, 2]), packet[:, :-1, 2]], axis=1)
    return jnp.stack([from_up_x, from_down_x, from_up_y, from_down_y], axis=2)

def apply_device(order_dev, velocity_dev, field_dev, links_dev, orient_dev, got_value, got_flux, got_visc, got_order, tables_all):
    live_modes, coef_u, coef_v = prepare(order_dev, velocity_dev, field_dev)
    strain_u, regular, viscosity, mean_visc = state_terms(coef_u, tables_all)
    volume = volume_terms(coef_v, strain_u, regular, viscosity, tables_all)
    local_value, local_slope = face_tables(coef_v, tables_all)
    recv_value = jnp.moveaxis(got_value, 0, 1).reshape(192, -1)
    recv_flux = jnp.moveaxis(got_flux, 0, 1).reshape(192, -1)
    faces = face_terms(local_value, local_slope, mean_visc, order_dev, links_dev, orient_dev, recv_value, recv_flux, got_visc.reshape(-1), got_order.reshape(-1), tables_all)
    return ((volume + faces) * live_modes).reshape(3, 512, order_dev.shape[0])

def reference(orders, velocity, adjoint_field, face_links, orient, send_faces):
    tables_all = basis_tables()
    devices = N_GX * N_GY

    def flatten_grid(array):
        return array.reshape((devices,) + array.shape[2:])

    def grid_back(array):
        return array.reshape((N_GX, N_GY) + array.shape[1:])

    def first_pass(items):
        return outgoing(items[0], items[1], items[2], items[3], tables_all)
    packets = lax.map(first_pass, (flatten_grid(orders), flatten_grid(velocity), flatten_grid(adjoint_field), flatten_grid(send_faces)))
    arrived = [flatten_grid(neighbour_view(grid_back(packet))) for packet in packets]

    def second_pass(items):
        return apply_device(items[0], items[1], items[2], items[3], items[4], items[5], items[6], items[7], items[8], tables_all)
    result = lax.map(second_pass, (flatten_grid(orders), flatten_grid(velocity), flatten_grid(adjoint_field), flatten_grid(face_links), flatten_grid(orient), arrived[0], arrived[1], arrived[2], arrived[3]))
    return grid_back(result)
```

```python
import functools

import jax
import jax.numpy as jnp
import numpy as np
from jax import lax
from jax.experimental import pallas as pl
from jax.experimental.pallas import tpu as pltpu
from jax.sharding import PartitionSpec as P

DELTA = 0.05
BF = jnp.bfloat16
F32 = jnp.float32
SLOPE = [i * (i + 1) / 2.0 for i in range(8)]
MASS = [2.0 / (2.0 * i + 1.0) for i in range(8)]
SYM = [[0, 3, 4], [3, 1, 5], [4, 5, 2]]


def split_np(x):
    hi = np.asarray(x, np.float32).astype(BF)
    lo = np.asarray(x - hi.astype(np.float64), np.float32).astype(BF)
    return hi, lo


@functools.cache
def tables():
    q = np.arange(8)
    x = np.cos(np.pi * (q + 0.5) / 8.0)
    w = np.pi / 8.0 * np.sqrt(1.0 - x * x)
    values, slopes = [np.ones(8), x], [np.zeros(8), np.ones(8)]
    for k in range(1, 7):
        values.append(((2 * k + 1) * x * values[k] - k * values[k - 1]) / (k + 1))
        slopes.append(slopes[k - 1] + (2 * k + 1) * values[k])
    leg, der = np.stack(values, 1), np.stack(slopes, 1)
    grads, divs = [], []
    for par in range(2):
        li, di = leg[:4, par::2], der[:4, par::2]
        full = np.concatenate(
            [
                np.kron(di, np.kron(leg, leg)),
                np.kron(li, np.kron(der, leg)),
                np.kron(li, np.kron(leg, der)),
            ],
            axis=0,
        )
        grads.append(np.concatenate(split_np(full), axis=1))
        divs.append(np.concatenate(split_np(full.T), axis=1))
    sign = (-1.0) ** q
    slope = np.array(SLOPE)
    eye = np.eye(64)
    ztrace = np.concatenate([np.kron(eye, v[None]) for v in (sign, np.ones(8), sign * slope, slope)], 0)
    even = (q % 2 == 0).astype(np.float64)
    odd = 1.0 - even
    zlift = np.concatenate([np.kron(eye, v[:, None]) for v in (even, odd, even * slope, odd * slope)], 1)
    wjk = np.broadcast_to(np.kron(w, w)[:, None], (64, 128))
    mass = np.array(MASS)
    mab = np.broadcast_to(np.kron(mass, mass)[:, None], (64, 128))
    return dict(
        grad=np.stack(grads),
        div=np.stack(divs),
        ztrace=ztrace.astype(BF),
        zlift=zlift.astype(BF),
        wjk=np.asarray(wjk, np.float32),
        mab=np.asarray(mab, np.float32),
        w=[float(v) for v in w],
        wsum=float(np.sum(w) ** 3),
    )


def dot(a, b):
    return jnp.dot(a, b, preferred_element_type=F32)


def split(x):
    hi = x.astype(BF)
    return hi, (x - hi.astype(F32)).astype(BF)


def level():
    row = lax.broadcasted_iota(jnp.int32, (64, 128), 0)
    return jnp.maximum(row // 8, row % 8)


def alive(lev, i, order):
    return jnp.maximum(lev, i) <= order


def masked_split(v_ref, order):
    lev = level()
    parts = [[[], []], [[], []]]
    for i in range(8):
        live = alive(lev, i, order)
        his, los = [], []
        for c in range(3):
            hi, lo = split(jnp.where(live, v_ref[pl.ds(c * 512 + i * 64, 64), :], 0.0))
            his.append(hi)
            los.append(lo)
        parts[i % 2][0].append(jnp.concatenate(his, axis=1))
        parts[i % 2][1].append(jnp.concatenate(los, axis=1))
    return [[jnp.concatenate(p, axis=0) for p in pp] for pp in parts]


def one_hot(first, count, target):
    row = lax.broadcasted_iota(jnp.int32, (count, 128), 0) + first
    return jnp.where(row == target, 1.0, 0.0).astype(BF)


def point_pair(ge, go, q, r0, rows):
    even, odd = {}, {}
    for d in range(3):
        for c in range(3):
            at = (pl.ds(pl.multiple_of(d * 256 + q * 64 + r0, 8), rows), pl.ds(c * 128, 128))
            even[d, c], odd[d, c] = ge[at], go[at]

    def strain(g):
        return [
            g[0, 0], g[1, 1], g[2, 2],
            0.5 * (g[0, 1] + g[1, 0]), 0.5 * (g[0, 2] + g[2, 0]), 0.5 * (g[1, 2] + g[2, 1]),
        ]

    near = {k: even[k] + odd[k] for k in even}
    far = {k: odd[k] - even[k] if k[0] == 0 else even[k] - odd[k] for k in even}
    return strain(near), strain(far)


def contract(a, b):
    return (a[0] * b[0] + a[1] * b[1] + a[2] * b[2]) + 2.0 * (a[3] * b[3] + a[4] * b[4] + a[5] * b[5])


def first_kernel(
    weights, wsum,
    order_ref, u_ref, v_ref, send_ref, par_ref, grad_ref, ztrace_ref, wjk_ref,
    eu_ref, ab_ref, own_ref, tab_ref, visc_ref, s0_ref, s1_ref, s2_ref, s3_ref,
    ge, go, vm,
):
    order = order_ref[...]
    lev = level()
    us = [[], []]
    for i in range(8):
        live = alive(lev, i, order)
        row = [
            jnp.where(live, u_ref[pl.ds(c * 512 + i * 64, 64), :].astype(F32), 0.0).astype(BF)
            for c in range(3)
        ]
        us[i % 2].append(jnp.concatenate(row, axis=1))
    for par, out in ((0, ge), (1, go)):
        u = jnp.concatenate(us[par], axis=0)
        out[...] = dot(grad_ref[par], jnp.concatenate([u, u], axis=0))

    for i in range(8):
        live = alive(lev, i, order)
        for c in range(3):
            at = pl.ds(c * 512 + i * 64, 64)
            vm[at, :] = jnp.where(live, v_ref[at, :], 0.0)

    total = jnp.zeros((8, 128), F32)
    for q in range(4):

        def points(m, acc, q=q):
            r0 = pl.multiple_of(m * 8, 8)
            w = wjk_ref[pl.ds(r0, 8), :] * weights[q]
            for at, e in zip((q, 7 - q), point_pair(ge, go, q, r0, 8)):
                inv = lax.rsqrt(2.0 * contract(e, e) + DELTA * DELTA)
                wmu = w + (2.0 * w) * inv
                acc = acc + wmu
                here = pl.multiple_of(at * 64 + r0, 8)
                for s in range(6):
                    eu_ref[pl.ds(s * 512 + here, 8), :] = e[s]
                ab_ref[pl.ds(here, 8), :] = 2.0 * wmu
                ab_ref[pl.ds(512 + here, 8), :] = (8.0 * w) * (inv * inv * inv)
            return acc

        total = lax.fori_loop(0, 8, points, total, unroll=2)
    visc = jnp.sum(total, axis=0, keepdims=True) * (1.0 / wsum)
    visc_ref[...] = jnp.broadcast_to(visc, (8, 128))

    def put(c, row, rows, d, even_v, odd_v, even_g, odd_g):
        for s in range(2):
            lanes = pl.ds((2 * d + s) * 128, 128)
            t = even_v + odd_v if s else even_v - odd_v
            g = even_g + odd_g if s else even_g - odd_g
            own_ref[pl.ds(c * 64 + row, rows), lanes] = t
            own_ref[pl.ds(192 + c * 64 + row, rows), lanes] = g * visc

    def sums(get):
        v = [get(i) for i in range(8)]
        return (
            (v[0] + v[2]) + (v[4] + v[6]),
            (v[1] + v[3]) + (v[5] + v[7]),
            (3.0 * v[2] + 10.0 * v[4]) + 21.0 * v[6],
            (v[1] + 6.0 * v[3]) + (15.0 * v[5] + 28.0 * v[7]),
        )

    for c in range(3):
        for m in range(8):
            put(c, m * 8, 8, 0, *sums(lambda i: vm[pl.ds(c * 512 + i * 64 + m * 8, 8), :]))
        for i in range(8):
            put(c, i * 8, 8, 1, *sums(lambda j: vm[pl.ds(c * 512 + i * 64 + j * 8, 8), :]))
    pieces = [split(vm[pl.ds(c * 512, 512), :]) for c in range(3)]
    both = jnp.concatenate([jnp.concatenate([p[k] for p in pieces], axis=1) for k in range(2)], axis=0)
    zt = ztrace_ref[...]
    z = dot(jnp.concatenate([zt, zt], axis=1), both)
    for c in range(3):
        for s in range(2):
            lanes = pl.ds((4 + s) * 128, 128)
            block = z[:, c * 128 : (c + 1) * 128]
            own_ref[pl.ds(c * 64, 64), lanes] = block[s * 64 : (s + 1) * 64]
            own_ref[pl.ds(192 + c * 64, 64), lanes] = block[128 + s * 64 : 192 + s * 64] * visc

    for f in range(6):
        lanes = pl.ds(f * 128, 128)
        for r in range(0, 384, 64):
            hi, lo = split(own_ref[pl.ds(r, 64), lanes])
            tab_ref[pl.ds(r, 64), lanes] = hi
            tab_ref[pl.ds(r, 64), pl.ds(768 + f * 128, 128)] = lo
    row = lax.broadcasted_iota(jnp.int32, (16, 128), 0)
    extra = jnp.where(row == 0, visc, jnp.where(row == 1, order.astype(F32), 0.0))
    hi, lo = split(extra)
    for f in range(6):
        tab_ref[pl.ds(384, 16), pl.ds(f * 128, 128)] = hi
        tab_ref[pl.ds(384, 16), pl.ds(768 + f * 128, 128)] = lo

    up_x, up_y = par_ref[0] == 0, par_ref[1] == 0
    rows = [send_ref[k : k + 1, :] for k in range(4)]
    picks = [
        jnp.where(up_y, rows[2], rows[3]),
        jnp.where(up_y, rows[3], rows[2]),
        jnp.where(up_x, rows[0], rows[1]),
        jnp.where(up_x, rows[1], rows[0]),
    ]
    hot = jnp.concatenate([one_hot(0, 768, p) for p in picks], axis=1)
    packet = dot(tab_ref[...], jnp.concatenate([hot, hot], axis=0))
    for k, out in enumerate((s0_ref, s1_ref, s2_ref, s3_ref)):
        out[...] = packet[:392, k * 128 : (k + 1) * 128]


def volume_kernel(
    order_ref, v_ref, eu_ref, ab_ref, grad_ref, div_ref, tab_ref, links_ref,
    vol_ref, far_ref,
    ge, go, sp,
):
    parts = masked_split(v_ref, order_ref[...])
    for par, out in ((0, ge), (1, go)):
        hi, lo = parts[par]
        mat = grad_ref[par]
        left = jnp.concatenate([mat[:, :256], mat], axis=1)
        out[...] = dot(left, jnp.concatenate([hi, lo, hi], axis=0))

    for q in range(4):

        def points(m, carry, q=q):
            r0 = pl.multiple_of(m * 16, 16)
            plus, minus = [[] for _ in range(6)], [[] for _ in range(6)]
            for half in range(2):
                rr = r0 + half * 8
                stress = []
                for at, ev in zip((q, 7 - q), point_pair(ge, go, q, rr, 8)):
                    here = pl.multiple_of(at * 64 + rr, 8)
                    eu = [eu_ref[pl.ds(s * 512 + here, 8), :] for s in range(6)]
                    a = ab_ref[pl.ds(here, 8), :]
                    b = ab_ref[pl.ds(512 + here, 8), :] * contract(eu, ev)
                    stress.append([a * ev[s] - b * eu[s] for s in range(6)])
                for s in range(6):
                    plus[s].append(stress[0][s] + stress[1][s])
                    minus[s].append(stress[0][s] - stress[1][s])
            for s in range(6):
                for k, value in enumerate((plus[s], minus[s])):
                    for j, piece in enumerate(split(jnp.concatenate(value, axis=0))):
                        base = ((s * 2 + k) * 2 + j) * 256 + q * 64
                        sp[pl.ds(pl.multiple_of(base + r0, 16), 16), :] = piece
            return carry

        lax.fori_loop(0, 4, points, 0)

    for par in range(2):
        halves = []
        for j in range(2):
            rows = []
            for d in range(3):
                k = (1 if d == 0 else 0) ^ par
                rows.append(
                    jnp.concatenate(
                        [sp[pl.ds(((SYM[d][c] * 2 + k) * 2 + j) * 256, 256), :] for c in range(3)], axis=1
                    )
                )
            halves.append(jnp.concatenate(rows, axis=0))
        mat = div_ref[par]
        left = jnp.concatenate([mat[:, :768], mat], axis=1)
        out = dot(left, jnp.concatenate([halves[0], halves[1], halves[0]], axis=0))
        for ii in range(4):
            for c in range(3):
                vol_ref[pl.ds(c * 512 + (2 * ii + par) * 64, 64), :] = out[
                    ii * 64 : ii * 64 + 64, c * 128 : c * 128 + 128
                ]

    hot = jnp.concatenate([one_hot(0, 768, links_ref[f : f + 1, :]) for f in range(6)], axis=1)
    far_ref[...] = dot(tab_ref[...], jnp.concatenate([hot, hot], axis=0))


def face_kernel(
    order_ref, far_ref, r0_ref, r1_ref, r2_ref, r3_ref, own_ref, visc_ref, links_ref, orient_ref, par_ref,
    vol_ref, zlift_ref, mab_ref,
    out_ref,
    got, acc, zin,
):
    order = order_ref[...]
    his, los = [], []
    for r in (r0_ref, r1_ref, r2_ref, r3_ref):
        hi, lo = split(jnp.concatenate([r[...], jnp.zeros((8, 128), F32)], axis=0))
        his.append(hi)
        los.append(lo)
    flip_x, flip_y = par_ref[0], par_ref[1]
    hots = []
    for f in range(6):
        link = links_ref[f : f + 1, :]
        slot = link - 768
        k = slot // 128
        block = jnp.where(k < 2, 2 + (k ^ flip_x), (k - 2) ^ flip_y)
        mapped = jnp.where((slot < 0) | (slot >= 512), -1, block * 128 + slot % 128)
        hots.append(one_hot(0, 512, mapped))
    hot = jnp.concatenate(hots, axis=1)
    left = jnp.concatenate(his + los, axis=1)
    got[...] = far_ref[...] + dot(left, jnp.concatenate([hot, hot], axis=0))

    visc = visc_ref[0:1, :]
    odd_b = lax.broadcasted_iota(jnp.int32, (8, 128), 0) % 2 == 1
    orderf = order.astype(F32)
    face = []
    for f in range(6):
        lanes = pl.ds(f * 128, 128)
        bits = orient_ref[f : f + 1, :]
        first = jnp.where(bits % 2 == 1, -1.0, 1.0)
        second = jnp.where(odd_b & (bits >= 2), -1.0, 1.0)
        spin = (second, second * first)
        far_visc, far_order = got[pl.ds(384, 1), lanes], got[pl.ds(385, 1), lanes]
        share = jnp.where(links_ref[f : f + 1, :] == 1280, 1.0, 0.5)
        top = jnp.maximum(orderf, far_order) + 1.0
        penalty = 2.0 * top * top * jnp.maximum(visc, far_visc)
        face.append((lanes, spin, share, penalty, share * visc))

    def flux(f, c, a):
        lanes, spin, share, penalty, weak = face[f]
        row, row_h = pl.ds(c * 64 + a * 8, 8), pl.ds(192 + c * 64 + a * 8, 8)
        rot = spin[a % 2]
        mm = mab_ref[pl.ds(a * 8, 8), :]
        jump = own_ref[row, lanes] - rot * got[row, lanes]
        value = mm * (penalty * jump - share * (own_ref[row_h, lanes] - rot * got[row_h, lanes]))
        return value, mm * (-weak * jump)

    def pair(d, c, a):
        v0, g0 = flux(2 * d, c, a)
        v1, g1 = flux(2 * d + 1, c, a)
        return v1 + v0, v1 - v0, g1 + g0, g1 - g0

    for c in range(3):
        for a in range(8):
            parts = pair(2, c, a)
            for k in range(4):
                zin[pl.ds(k * 64 + a * 8, 8), pl.ds(c * 128, 128)] = parts[k]
    hi, lo = split(zin[...])
    zl = zlift_ref[...]
    acc[...] = dot(jnp.concatenate([zl, zl], axis=1), jnp.concatenate([hi, lo], axis=0))

    lev = level()
    for c in range(3):
        lanes = pl.ds(c * 128, 128)
        for a in range(8):
            ve, vo, ge, go = pair(1, c, a)
            for j in range(8):
                at = pl.ds(a * 64 + j * 8, 8)
                acc[at, lanes] = acc[at, lanes] + ((vo + SLOPE[j] * go) if j % 2 else (ve + SLOPE[j] * ge))
        for a in range(8):
            ve, vo, ge, go = pair(0, c, a)
            for i in range(8):
                at = pl.ds(i * 64 + a * 8, 8)
                to = pl.ds(c * 512 + i * 64 + a * 8, 8)
                value = acc[at, lanes] + ((vo + SLOPE[i] * go) if i % 2 else (ve + SLOPE[i] * ge))
                live = alive(lev[a * 8 : a * 8 + 8], i, order)
                out_ref[to, :] = jnp.where(live, vol_ref[to, :] + value, 0.0)


def shape(rows, cols=128, kind=F32):
    return jax.ShapeDtypeStruct((rows, cols), kind)


VM = pl.BlockSpec(memory_space=pltpu.VMEM)
SM = pl.BlockSpec(memory_space=pltpu.SMEM)


def pairs(count, first):
    return [p for s in range(first, count - 1, 2) for p in ((s, s + 1), (s + 1, s))]


def exchange(value, axis, first):
    return lax.ppermute(value, axis, pairs(lax.axis_size(axis), first))


def body(orders, velocity, adjoint_field, face_links, orient, send_faces):
    tab = tables()
    order = orders[0]
    u = velocity.reshape(1536, 128)
    v = adjoint_field.reshape(1536, 128)
    par = jnp.stack([lax.axis_index("gx") % 2, lax.axis_index("gy") % 2]).astype(jnp.int32)
    grad, div = jnp.asarray(tab["grad"]), jnp.asarray(tab["div"])
    eu, ab, own, table, visc, *packets = pl.pallas_call(
        functools.partial(first_kernel, tab["w"], tab["wsum"]),
        out_shape=[shape(3072), shape(1024), shape(384, 768), shape(400, 1536, BF), shape(8)] + [shape(392)] * 4,
        in_specs=[VM, VM, VM, VM, SM, VM, VM, VM],
        out_specs=[VM] * 9,
        scratch_shapes=[pltpu.VMEM((768, 384), F32), pltpu.VMEM((768, 384), F32), pltpu.VMEM((1536, 128), F32)],
        name="state_and_traces",
    )(order, u, v, send_faces[0, 0], par, grad, jnp.asarray(tab["ztrace"]), jnp.asarray(tab["wjk"]))
    got = [
        exchange(packets[0], "gy", 0),
        exchange(packets[1], "gy", 1),
        exchange(packets[2], "gx", 0),
        exchange(packets[3], "gx", 1),
    ]
    vol, far = pl.pallas_call(
        volume_kernel,
        out_shape=[shape(1536), shape(400, 768)],
        in_specs=[VM] * 8,
        out_specs=[VM] * 2,
        scratch_shapes=[pltpu.VMEM((768, 384), F32), pltpu.VMEM((768, 384), F32), pltpu.VMEM((6144, 128), BF)],
        name="volume",
    )(order, v, eu, ab, grad, div, table, face_links[0, 0])
    out = pl.pallas_call(
        face_kernel,
        out_shape=shape(1536),
        in_specs=[VM] * 10 + [SM] + [VM] * 3,
        out_specs=VM,
        scratch_shapes=[pltpu.VMEM((400, 768), F32), pltpu.VMEM((512, 384), F32), pltpu.VMEM((256, 384), F32)],
        name="faces",
    )(
        order, far, *got, own, visc, face_links[0, 0], orient[0, 0], par, vol,
        jnp.asarray(tab["zlift"]), jnp.asarray(tab["mab"]),
    )
    return out.reshape(1, 1, 3, 512, 128)


def solution(mesh):
    return jax.shard_map(
        body,
        mesh=mesh,
        in_specs=(
            P("gx", "gy", None),
            P("gx", "gy", None, None, None),
            P("gx", "gy", None, None, None),
            P("gx", "gy", None, None),
            P("gx", "gy", None, None),
            P("gx", "gy", None, None),
        ),
        out_specs=P("gx", "gy", None, None, None),
        check_vma=False,
    )
```

```python
import functools

import jax
import jax.numpy as jnp
import numpy as np
from jax import lax
from jax.experimental import pallas as pl
from jax.experimental.pallas import tpu as pltpu
from jax.sharding import PartitionSpec as P

DELTA = 0.05
BF = jnp.bfloat16
F32 = jnp.float32
SLOPE = [i * (i + 1) / 2.0 for i in range(8)]
MASS = [2.0 / (2.0 * i + 1.0) for i in range(8)]
SYM = [[0, 3, 4], [3, 1, 5], [4, 5, 2]]


def split_np(x):
    hi = np.asarray(x, np.float32).astype(BF)
    lo = np.asarray(x - hi.astype(np.float64), np.float32).astype(BF)
    return hi, lo


@functools.cache
def tables():
    q = np.arange(8)
    x = np.cos(np.pi * (q + 0.5) / 8.0)
    w = np.pi / 8.0 * np.sqrt(1.0 - x * x)
    values, slopes = [np.ones(8), x], [np.zeros(8), np.ones(8)]
    for k in range(1, 7):
        values.append(((2 * k + 1) * x * values[k] - k * values[k - 1]) / (k + 1))
        slopes.append(slopes[k - 1] + (2 * k + 1) * values[k])
    leg, der = np.stack(values, 1), np.stack(slopes, 1)
    grads, divs = [], []
    for par in range(2):
        li, di = leg[:4, par::2], der[:4, par::2]
        full = np.concatenate(
            [
                np.kron(di, np.kron(leg, leg)),
                np.kron(li, np.kron(der, leg)),
                np.kron(li, np.kron(leg, der)),
            ],
            axis=0,
        )
        grads.append(np.concatenate(split_np(full), axis=1))
        divs.append(np.concatenate(split_np(full.T), axis=1))
    sign = (-1.0) ** q
    slope = np.array(SLOPE)
    eye = np.eye(64)
    ztrace = np.concatenate([np.kron(eye, v[None]) for v in (sign, np.ones(8), sign * slope, slope)], 0)
    even = (q % 2 == 0).astype(np.float64)
    odd = 1.0 - even
    zlift = np.concatenate([np.kron(eye, v[:, None]) for v in (even, odd, even * slope, odd * slope)], 1)
    wjk = np.broadcast_to(np.kron(w, w)[:, None], (64, 128))
    mass = np.array(MASS)
    mab = np.broadcast_to(np.kron(mass, mass)[:, None], (64, 128))
    return dict(
        grad=np.stack(grads),
        div=np.stack(divs),
        ztrace=ztrace.astype(BF),
        zlift=zlift.astype(BF),
        wjk=np.asarray(wjk, np.float32),
        mab=np.asarray(mab, np.float32),
        w=[float(v) for v in w],
        wsum=float(np.sum(w) ** 3),
    )


def dot(a, b):
    return jnp.dot(a, b, preferred_element_type=F32)


def split(x):
    hi = x.astype(BF)
    return hi, (x - hi.astype(F32)).astype(BF)


def level():
    row = lax.broadcasted_iota(jnp.int32, (64, 128), 0)
    return jnp.maximum(row // 8, row % 8)


def alive(lev, i, order):
    return jnp.maximum(lev, i) <= order


def one_hot(first, count, target):
    row = lax.broadcasted_iota(jnp.int32, (count, 128), 0) + first
    return jnp.where(row == target, 1.0, 0.0).astype(BF)


def point_pair(ge, go, q, r0, rows):
    even, odd = {}, {}
    for d in range(3):
        for c in range(3):
            at = (pl.ds(pl.multiple_of(d * 256 + q * 64 + r0, 8), rows), pl.ds(c * 128, 128))
            even[d, c], odd[d, c] = ge[at], go[at]

    def strain(g):
        return [
            g[0, 0], g[1, 1], g[2, 2],
            0.5 * (g[0, 1] + g[1, 0]), 0.5 * (g[0, 2] + g[2, 0]), 0.5 * (g[1, 2] + g[2, 1]),
        ]

    near = {k: even[k] + odd[k] for k in even}
    far = {k: odd[k] - even[k] if k[0] == 0 else even[k] - odd[k] for k in even}
    return strain(near), strain(far)


def contract(a, b):
    return (a[0] * b[0] + a[1] * b[1] + a[2] * b[2]) + 2.0 * (a[3] * b[3] + a[4] * b[4] + a[5] * b[5])


def first_kernel(
    weights, wsum,
    order_hbm, u_hbm, v_hbm, send_hbm, grad_hbm, ztrace_hbm, wjk_hbm,
    eu_ref, ab_ref, own_ref, tab_ref, visc_ref, vhi_ref, vlo_ref, s0_ref, s1_ref, s2_ref, s3_ref,
    order_ref, u_ref, v_ref, send_ref, grad_ref, ztrace_ref, wjk_ref, ge, go, vm, sems,
):
    names = ("order", "u", "grad", "v", "wjk", "ztrace", "send")
    ends = (
        (order_hbm, order_ref), (u_hbm, u_ref), (grad_hbm, grad_ref), (v_hbm, v_ref),
        (wjk_hbm, wjk_ref), (ztrace_hbm, ztrace_ref), (send_hbm, send_ref),
    )
    loads = {n: pltpu.make_async_copy(*e, sems.at[k]) for k, (n, e) in enumerate(zip(names, ends))}
    for n in names:
        loads[n].start()
    loads["order"].wait()
    loads["u"].wait()
    order = order_ref[...]
    lev = level()
    us = [[], []]
    for i in range(8):
        live = alive(lev, i, order)
        row = [
            jnp.where(live, u_ref[pl.ds(c * 512 + i * 64, 64), :].astype(F32), 0.0).astype(BF)
            for c in range(3)
        ]
        us[i % 2].append(jnp.concatenate(row, axis=1))
    loads["grad"].wait()
    for par, out in ((0, ge), (1, go)):
        u = jnp.concatenate(us[par], axis=0)
        out[...] = dot(grad_ref[par], jnp.concatenate([u, u], axis=0))

    loads["v"].wait()
    loads["wjk"].wait()
    loads["ztrace"].wait()
    loads["send"].wait()
    for i in range(8):
        live = alive(lev, i, order)
        for c in range(3):
            at = pl.ds(c * 512 + i * 64, 64)
            value = jnp.where(live, v_ref[at, :], 0.0)
            vm[at, :] = value
            vhi_ref[at, :], vlo_ref[at, :] = split(value)

    total = jnp.zeros((8, 128), F32)
    for q in range(4):

        def points(m, acc, q=q):
            r0 = pl.multiple_of(m * 8, 8)
            w = wjk_ref[pl.ds(r0, 8), :] * weights[q]
            for at, e in zip((q, 7 - q), point_pair(ge, go, q, r0, 8)):
                inv = lax.rsqrt(2.0 * contract(e, e) + DELTA * DELTA)
                wmu = w + (2.0 * w) * inv
                acc = acc + wmu
                here = pl.multiple_of(at * 64 + r0, 8)
                for s in range(6):
                    eu_ref[pl.ds(s * 512 + here, 8), :] = e[s]
                ab_ref[pl.ds(here, 8), :] = 2.0 * wmu
                ab_ref[pl.ds(512 + here, 8), :] = (8.0 * w) * (inv * inv * inv)
            return acc

        total = lax.fori_loop(0, 8, points, total, unroll=2)
    visc = jnp.sum(total, axis=0, keepdims=True) * (1.0 / wsum)
    visc_ref[...] = jnp.broadcast_to(visc, (8, 128))

    def put(c, row, rows, d, even_v, odd_v, even_g, odd_g):
        for s in range(2):
            lanes = pl.ds((2 * d + s) * 128, 128)
            t = even_v + odd_v if s else even_v - odd_v
            g = even_g + odd_g if s else even_g - odd_g
            own_ref[pl.ds(c * 64 + row, rows), lanes] = t
            own_ref[pl.ds(192 + c * 64 + row, rows), lanes] = g * visc

    def sums(get):
        v = [get(i) for i in range(8)]
        return (
            (v[0] + v[2]) + (v[4] + v[6]),
            (v[1] + v[3]) + (v[5] + v[7]),
            (3.0 * v[2] + 10.0 * v[4]) + 21.0 * v[6],
            (v[1] + 6.0 * v[3]) + (15.0 * v[5] + 28.0 * v[7]),
        )

    for c in range(3):
        for m in range(8):
            put(c, m * 8, 8, 0, *sums(lambda i: vm[pl.ds(c * 512 + i * 64 + m * 8, 8), :]))
        for i in range(8):
            put(c, i * 8, 8, 1, *sums(lambda j: vm[pl.ds(c * 512 + i * 64 + j * 8, 8), :]))
    both = jnp.concatenate(
        [jnp.concatenate([r[pl.ds(c * 512, 512), :] for c in range(3)], axis=1) for r in (vhi_ref, vlo_ref)], axis=0
    )
    zt = ztrace_ref[...]
    z = dot(jnp.concatenate([zt, zt], axis=1), both)
    for c in range(3):
        for s in range(2):
            lanes = pl.ds((4 + s) * 128, 128)
            block = z[:, c * 128 : (c + 1) * 128]
            own_ref[pl.ds(c * 64, 64), lanes] = block[s * 64 : (s + 1) * 64]
            own_ref[pl.ds(192 + c * 64, 64), lanes] = block[128 + s * 64 : 192 + s * 64] * visc

    for f in range(6):
        lanes = pl.ds(f * 128, 128)
        for r in range(0, 384, 64):
            hi, lo = split(own_ref[pl.ds(r, 64), lanes])
            tab_ref[pl.ds(r, 64), lanes] = hi
            tab_ref[pl.ds(r, 64), pl.ds(768 + f * 128, 128)] = lo
    row = lax.broadcasted_iota(jnp.int32, (16, 128), 0)
    extra = jnp.where(row == 0, visc, jnp.where(row == 1, order.astype(F32), 0.0))
    hi, lo = split(extra)
    for f in range(6):
        tab_ref[pl.ds(384, 16), pl.ds(f * 128, 128)] = hi
        tab_ref[pl.ds(384, 16), pl.ds(768 + f * 128, 128)] = lo

    up_x, up_y = lax.axis_index("gx") % 2 == 0, lax.axis_index("gy") % 2 == 0
    rows = [send_ref[0, 0, k : k + 1, :] for k in range(4)]
    picks = [
        jnp.where(up_y, rows[2], rows[3]),
        jnp.where(up_y, rows[3], rows[2]),
        jnp.where(up_x, rows[0], rows[1]),
        jnp.where(up_x, rows[1], rows[0]),
    ]
    hot = jnp.concatenate([one_hot(0, 768, p) for p in picks], axis=1)
    packet = dot(tab_ref[...], jnp.concatenate([hot, hot], axis=0))
    for k, out in enumerate((s0_ref, s1_ref, s2_ref, s3_ref)):
        out[...] = packet[:392, k * 128 : (k + 1) * 128]


def volume_kernel(
    vhi_ref, vlo_ref, eu_ref, ab_ref, grad_ref, div_hbm, tab_ref, links_ref,
    vol_ref, far_ref,
    div_ref, ge, go, sp, sem,
):
    load = pltpu.make_async_copy(div_hbm, div_ref, sem)
    load.start()
    for par, out in ((0, ge), (1, go)):
        hi, lo = (
            jnp.concatenate(
                [
                    jnp.concatenate([r[pl.ds(c * 512 + i * 64, 64), :] for c in range(3)], axis=1)
                    for i in range(par, 8, 2)
                ],
                axis=0,
            )
            for r in (vhi_ref, vlo_ref)
        )
        mat = grad_ref[par]
        left = jnp.concatenate([mat[:, :256], mat], axis=1)
        out[...] = dot(left, jnp.concatenate([hi, lo, hi], axis=0))

    for q in range(4):

        def points(m, carry, q=q):
            r0 = pl.multiple_of(m * 16, 16)
            plus, minus = [[] for _ in range(6)], [[] for _ in range(6)]
            for half in range(2):
                rr = r0 + half * 8
                stress = []
                for at, ev in zip((q, 7 - q), point_pair(ge, go, q, rr, 8)):
                    here = pl.multiple_of(at * 64 + rr, 8)
                    eu = [eu_ref[pl.ds(s * 512 + here, 8), :] for s in range(6)]
                    a = ab_ref[pl.ds(here, 8), :]
                    b = ab_ref[pl.ds(512 + here, 8), :] * contract(eu, ev)
                    stress.append([a * ev[s] - b * eu[s] for s in range(6)])
                for s in range(6):
                    plus[s].append(stress[0][s] + stress[1][s])
                    minus[s].append(stress[0][s] - stress[1][s])
            for s in range(6):
                for k, value in enumerate((plus[s], minus[s])):
                    for j, piece in enumerate(split(jnp.concatenate(value, axis=0))):
                        base = ((s * 2 + k) * 2 + j) * 256 + q * 64
                        sp[pl.ds(pl.multiple_of(base + r0, 16), 16), :] = piece
            return carry

        lax.fori_loop(0, 4, points, 0)

    load.wait()
    for par in range(2):
        halves = []
        for j in range(2):
            rows = []
            for d in range(3):
                k = (1 if d == 0 else 0) ^ par
                rows.append(
                    jnp.concatenate(
                        [sp[pl.ds(((SYM[d][c] * 2 + k) * 2 + j) * 256, 256), :] for c in range(3)], axis=1
                    )
                )
            halves.append(jnp.concatenate(rows, axis=0))
        mat = div_ref[par]
        left = jnp.concatenate([mat[:, :768], mat], axis=1)
        out = dot(left, jnp.concatenate([halves[0], halves[1], halves[0]], axis=0))
        for ii in range(4):
            for c in range(3):
                vol_ref[pl.ds(c * 512 + (2 * ii + par) * 64, 64), :] = out[
                    ii * 64 : ii * 64 + 64, c * 128 : c * 128 + 128
                ]

    hot = jnp.concatenate([one_hot(0, 768, links_ref[f]) for f in range(6)], axis=1)
    far_ref[...] = dot(tab_ref[...], jnp.concatenate([hot, hot], axis=0))


def face_kernel(
    order_ref, far_ref, r0_ref, r1_ref, r2_ref, r3_ref, own_ref, visc_ref, links_ref, orient_ref,
    vol_ref, zlift_ref, mab_ref,
    out_ref,
    got, acc, zin,
):
    order = order_ref[...]
    his, los = [], []
    for r in (r0_ref, r1_ref, r2_ref, r3_ref):
        hi, lo = split(jnp.concatenate([r[...], jnp.zeros((8, 128), F32)], axis=0))
        his.append(hi)
        los.append(lo)
    flip_x, flip_y = lax.axis_index("gx") % 2, lax.axis_index("gy") % 2
    hots = []
    for f in range(6):
        link = links_ref[f]
        slot = link - 768
        k = slot // 128
        block = jnp.where(k < 2, 2 + (k ^ flip_x), (k - 2) ^ flip_y)
        mapped = jnp.where((slot < 0) | (slot >= 512), -1, block * 128 + slot % 128)
        hots.append(one_hot(0, 512, mapped))
    hot = jnp.concatenate(hots, axis=1)
    left = jnp.concatenate(his + los, axis=1)
    got[...] = far_ref[...] + dot(left, jnp.concatenate([hot, hot], axis=0))

    visc = visc_ref[0:1, :]
    odd_b = lax.broadcasted_iota(jnp.int32, (8, 128), 0) % 2 == 1
    orderf = order.astype(F32)
    face = []
    for f in range(6):
        lanes = pl.ds(f * 128, 128)
        bits = orient_ref[f]
        first = jnp.where(bits % 2 == 1, -1.0, 1.0)
        second = jnp.where(odd_b & (bits >= 2), -1.0, 1.0)
        spin = (second, second * first)
        far_visc, far_order = got[pl.ds(384, 1), lanes], got[pl.ds(385, 1), lanes]
        share = jnp.where(links_ref[f] == 1280, 1.0, 0.5)
        top = jnp.maximum(orderf, far_order) + 1.0
        penalty = 2.0 * top * top * jnp.maximum(visc, far_visc)
        face.append((lanes, spin, share, penalty, share * visc))

    def flux(f, c, a):
        lanes, spin, share, penalty, weak = face[f]
        row, row_h = pl.ds(c * 64 + a * 8, 8), pl.ds(192 + c * 64 + a * 8, 8)
        rot = spin[a % 2]
        mm = mab_ref[pl.ds(a * 8, 8), :]
        jump = own_ref[row, lanes] - rot * got[row, lanes]
        value = mm * (penalty * jump - share * (own_ref[row_h, lanes] - rot * got[row_h, lanes]))
        return value, mm * (-weak * jump)

    def pair(d, c, a):
        v0, g0 = flux(2 * d, c, a)
        v1, g1 = flux(2 * d + 1, c, a)
        return v1 + v0, v1 - v0, g1 + g0, g1 - g0

    for c in range(3):
        for a in range(8):
            parts = pair(2, c, a)
            for k in range(4):
                zin[pl.ds(k * 64 + a * 8, 8), pl.ds(c * 128, 128)] = parts[k]
    hi, lo = split(zin[...])
    zl = zlift_ref[...]
    acc[...] = dot(jnp.concatenate([zl, zl], axis=1), jnp.concatenate([hi, lo], axis=0))

    lev = level()
    for c in range(3):
        lanes = pl.ds(c * 128, 128)
        for a in range(8):
            ve, vo, ge, go = pair(1, c, a)
            for j in range(8):
                at = pl.ds(a * 64 + j * 8, 8)
                acc[at, lanes] = acc[at, lanes] + ((vo + SLOPE[j] * go) if j % 2 else (ve + SLOPE[j] * ge))
        for a in range(8):
            ve, vo, ge, go = pair(0, c, a)
            for i in range(8):
                at = pl.ds(i * 64 + a * 8, 8)
                to = pl.ds(c * 512 + i * 64 + a * 8, 8)
                value = acc[at, lanes] + ((vo + SLOPE[i] * go) if i % 2 else (ve + SLOPE[i] * ge))
                live = alive(lev[a * 8 : a * 8 + 8], i, order)
                out_ref[to, :] = jnp.where(live, vol_ref[to, :] + value, 0.0)


def shape(rows, cols=128, kind=F32):
    return jax.ShapeDtypeStruct((rows, cols), kind)


VM = pl.BlockSpec(memory_space=pltpu.VMEM)
HBM = pl.BlockSpec(memory_space=pltpu.HBM)
PARAMS = pltpu.CompilerParams(vmem_limit_bytes=20 * 1024 * 1024)


def partner(s, count, first):
    t = s + 1 if (s - first) % 2 == 0 else s - 1
    return t if first <= min(s, t) and max(s, t) < count else None


def exchange(value, axis, first):
    gx, gy = lax.axis_size("gx"), lax.axis_size("gy")
    links = []
    for x in range(gx):
        for y in range(gy):
            if axis == "gx":
                tx, ty = partner(x, gx, first), y
                if tx is None:
                    tx, ty = x, partner(y, gy, 0)
                    ty = y if ty is None else ty
            else:
                tx, ty = x, partner(y, gy, first)
                if ty is None:
                    ty = gy - 1 - y if gy % 2 == 0 else y
            links.append((x * gy + y, tx * gy + ty))
    return lax.ppermute(value, ("gx", "gy"), links)


def in_hbm(x):
    return pltpu.with_memory_space_constraint(x, pltpu.HBM)


def body(orders, velocity, adjoint_field, face_links, orient, send_faces):
    tab = tables()
    order = orders[0]
    u = velocity.reshape(1536, 128)
    v = adjoint_field.reshape(1536, 128)
    grad, div = jnp.asarray(tab["grad"]), jnp.asarray(tab["div"])
    links, turns = face_links.reshape(6, 1, 128), orient.reshape(6, 1, 128)
    eu, ab, own, table, visc, vhi, vlo, *packets = pl.pallas_call(
        functools.partial(first_kernel, tab["w"], tab["wsum"]),
        out_shape=[shape(3072), shape(1024), shape(384, 768), shape(400, 1536, BF), shape(8)]
        + [shape(1536, 128, BF)] * 2
        + [shape(392)] * 4,
        in_specs=[HBM] * 7,
        out_specs=[VM] * 11,
        scratch_shapes=[
            pltpu.VMEM((1, 128), jnp.int32),
            pltpu.VMEM((1536, 128), BF),
            pltpu.VMEM((1536, 128), F32),
            pltpu.VMEM((1, 1, 4, 128), jnp.int32),
            pltpu.VMEM((2, 768, 512), BF),
            pltpu.VMEM((256, 512), BF),
            pltpu.VMEM((64, 128), F32),
            pltpu.VMEM((768, 384), F32),
            pltpu.VMEM((768, 384), F32),
            pltpu.VMEM((1536, 128), F32),
            pltpu.SemaphoreType.DMA((7,)),
        ],
        compiler_params=PARAMS,
        name="state_and_traces",
    )(*map(in_hbm, (order, u, v, send_faces, grad, jnp.asarray(tab["ztrace"]), jnp.asarray(tab["wjk"]))))
    got = [
        exchange(packets[0], "gy", 0),
        exchange(packets[1], "gy", 1),
        exchange(packets[2], "gx", 0),
        exchange(packets[3], "gx", 1),
    ]
    vol, far = pl.pallas_call(
        volume_kernel,
        out_shape=[shape(1536), shape(400, 768)],
        in_specs=[VM] * 5 + [HBM] + [VM] * 2,
        out_specs=[VM] * 2,
        scratch_shapes=[pltpu.VMEM((2, 256, 1536), BF), pltpu.VMEM((768, 384), F32), pltpu.VMEM((768, 384), F32), pltpu.VMEM((6144, 128), BF), pltpu.SemaphoreType.DMA],
        compiler_params=PARAMS,
        name="volume",
    )(vhi, vlo, eu, ab, grad, in_hbm(div), table, links)
    out = pl.pallas_call(
        face_kernel,
        out_shape=shape(1536),
        in_specs=[VM] * 13,
        out_specs=VM,
        scratch_shapes=[pltpu.VMEM((400, 768), F32), pltpu.VMEM((512, 384), F32), pltpu.VMEM((256, 384), F32)],
        compiler_params=PARAMS,
        name="faces",
    )(
        order, far, *got, own, visc, links, turns, vol,
        jnp.asarray(tab["zlift"]), jnp.asarray(tab["mab"]),
    )
    return out.reshape(1, 1, 3, 512, 128)


def solution(mesh):
    return jax.shard_map(
        body,
        mesh=mesh,
        in_specs=(
            P("gx", "gy", None),
            P("gx", "gy", None, None, None),
            P("gx", "gy", None, None, None),
            P("gx", "gy", None, None),
            P("gx", "gy", None, None),
            P("gx", "gy", None, None),
        ),
        out_specs=P("gx", "gy", None, None, None),
        check_vma=False,
    )
```

```python
import functools

import jax
import jax.numpy as jnp
import numpy as np
from jax import lax
from jax.experimental import pallas as pl
from jax.experimental.pallas import tpu as pltpu
from jax.sharding import PartitionSpec as P

DELTA = 0.05
BF = jnp.bfloat16
F32 = jnp.float32
MXU_ROWS = 256
SLOPE = [i * (i + 1) / 2.0 for i in range(8)]
MASS = [2.0 / (2.0 * i + 1.0) for i in range(8)]
SYM = [[0, 3, 4], [3, 1, 5], [4, 5, 2]]


def split_np(x):
    hi = np.asarray(x, np.float32).astype(BF)
    lo = np.asarray(x - hi.astype(np.float64), np.float32).astype(BF)
    return hi, lo


@functools.cache
def tables():
    q = np.arange(8)
    x = np.cos(np.pi * (q + 0.5) / 8.0)
    w = np.pi / 8.0 * np.sqrt(1.0 - x * x)
    values, slopes = [np.ones(8), x], [np.zeros(8), np.ones(8)]
    for k in range(1, 7):
        values.append(((2 * k + 1) * x * values[k] - k * values[k - 1]) / (k + 1))
        slopes.append(slopes[k - 1] + (2 * k + 1) * values[k])
    leg, der = np.stack(values, 1), np.stack(slopes, 1)
    grads, divs = [], []
    for par in range(2):
        li, di = leg[:4, par::2], der[:4, par::2]
        full = np.concatenate(
            [
                np.kron(di, np.kron(leg, leg)),
                np.kron(li, np.kron(der, leg)),
                np.kron(li, np.kron(leg, der)),
            ],
            axis=0,
        )
        grads.append(np.concatenate(split_np(full), axis=1))
        divs.append(np.concatenate(split_np(full.T), axis=1))
    sign = (-1.0) ** q
    slope = np.array(SLOPE)
    eye = np.eye(64)
    ztrace = np.concatenate([np.kron(eye, v[None]) for v in (sign, np.ones(8), sign * slope, slope)], 0)
    even = (q % 2 == 0).astype(np.float64)
    odd = 1.0 - even
    zlift = np.concatenate([np.kron(eye, v[:, None]) for v in (even, odd, even * slope, odd * slope)], 1)
    wjk = np.broadcast_to(np.kron(w, w)[:, None], (64, 128))
    mass = np.array(MASS)
    mab = np.broadcast_to(np.kron(mass, mass)[:, None], (64, 128))
    return dict(
        grad=np.stack(grads),
        div=np.stack(divs),
        ztrace=ztrace.astype(BF),
        zlift=zlift.astype(BF),
        wjk=np.asarray(wjk, np.float32),
        mab=np.asarray(mab, np.float32),
        w=[float(v) for v in w],
        wsum=float(np.sum(w) ** 3),
    )


def dot(a, b):
    return jnp.dot(a, b, preferred_element_type=F32)


def split(x):
    hi = x.astype(BF)
    return hi, (x - hi.astype(F32)).astype(BF)


def level():
    row = lax.broadcasted_iota(jnp.int32, (64, 128), 0)
    return jnp.maximum(row // 8, row % 8)


def alive(lev, i, order):
    return jnp.maximum(lev, i) <= order


def lane_pick(get, count, target):
    low, tile = target & 127, target >> 7
    out = jnp.zeros(target.shape, F32)
    for t in range(count):
        out = jnp.where(tile == t, jnp.take_along_axis(get(t), low, axis=1), out)
    return out


def point_pair(ge, go, q, r0, rows):
    even, odd = {}, {}
    for d in range(3):
        for c in range(3):
            at = (pl.ds(pl.multiple_of(d * 256 + q * 64 + r0, 8), rows), pl.ds(c * 128, 128))
            even[d, c], odd[d, c] = ge[at], go[at]

    def strain(g):
        return [
            g[0, 0], g[1, 1], g[2, 2],
            0.5 * (g[0, 1] + g[1, 0]), 0.5 * (g[0, 2] + g[2, 0]), 0.5 * (g[1, 2] + g[2, 1]),
        ]

    near = {k: even[k] + odd[k] for k in even}
    far = {k: odd[k] - even[k] if k[0] == 0 else even[k] - odd[k] for k in even}
    return strain(near), strain(far)


def contract(a, b):
    return (a[0] * b[0] + a[1] * b[1] + a[2] * b[2]) + 2.0 * (a[3] * b[3] + a[4] * b[4] + a[5] * b[5])


def first_kernel(
    weights, wsum,
    order_hbm, u_hbm, v_hbm, send_hbm, grad_hbm, ztrace_hbm, wjk_hbm,
    eu_ref, ab_ref, own_ref, extra_ref, vhi_ref, vlo_ref, grad_ref, g0_ref, s0_ref, s1_ref, s2_ref, s3_ref,
    order_ref, u_ref, v_ref, send_ref, ztrace_ref, wjk_ref, ge, go, sems,
):
    names = ("order", "v", "ztrace", "u", "grad", "send", "wjk")
    ends = (
        (order_hbm, order_ref), (v_hbm, v_ref), (ztrace_hbm, ztrace_ref), (u_hbm, u_ref), (grad_hbm, grad_ref),
        (send_hbm, send_ref), (wjk_hbm, wjk_ref),
    )
    loads = {n: pltpu.make_async_copy(*e, sems.at[k]) for k, (n, e) in enumerate(zip(names, ends))}
    for n in names:
        loads[n].start()
    loads["order"].wait()
    order = order_ref[...]
    lev = level()
    loads["v"].wait()
    for i in range(8):
        live = alive(lev, i, order)
        for c in range(3):
            at = pl.ds(c * 512 + i * 64, 64)
            value = jnp.where(live, v_ref[at, :], 0.0)
            v_ref[at, :] = value
            vhi_ref[at, :], vlo_ref[at, :] = split(value)

    def put(c, row, rows, d, even_v, odd_v, even_g, odd_g):
        for s in range(2):
            lanes = pl.ds((2 * d + s) * 128, 128)
            own_ref[pl.ds(c * 64 + row, rows), lanes] = even_v + odd_v if s else even_v - odd_v
            own_ref[pl.ds(192 + c * 64 + row, rows), lanes] = even_g + odd_g if s else even_g - odd_g

    def sums(get):
        v = [get(i) for i in range(8)]
        return (
            (v[0] + v[2]) + (v[4] + v[6]),
            (v[1] + v[3]) + (v[5] + v[7]),
            (3.0 * v[2] + 10.0 * v[4]) + 21.0 * v[6],
            (v[1] + 6.0 * v[3]) + (15.0 * v[5] + 28.0 * v[7]),
        )

    for c in range(3):
        for m in range(8):
            put(c, m * 8, 8, 0, *sums(lambda i: v_ref[pl.ds(c * 512 + i * 64 + m * 8, 8), :]))
        for i in range(8):
            put(c, i * 8, 8, 1, *sums(lambda j: v_ref[pl.ds(c * 512 + i * 64 + j * 8, 8), :]))
    loads["ztrace"].wait()
    both = jnp.concatenate([r[pl.ds(c * 512, 512), :] for r in (vhi_ref, vlo_ref) for c in range(3)], axis=1)
    z = dot(ztrace_ref[...], both)
    for c in range(3):
        block = z[:, c * 128 : (c + 1) * 128] + z[:, 384 + c * 128 : 512 + c * 128]
        for s in range(2):
            lanes = pl.ds((4 + s) * 128, 128)
            own_ref[pl.ds(c * 64, 64), lanes] = block[s * 64 : (s + 1) * 64]
            own_ref[pl.ds(192 + c * 64, 64), lanes] = block[128 + s * 64 : 192 + s * 64]

    for n in ("u", "grad", "send", "wjk"):
        loads[n].wait()
    us = [[], []]
    for i in range(8):
        live = alive(lev, i, order)
        row = [
            jnp.where(live, u_ref[pl.ds(c * 512 + i * 64, 64), :].astype(F32), 0.0).astype(BF)
            for c in range(3)
        ]
        us[i % 2].append(jnp.concatenate(row + [vhi_ref[pl.ds(i * 64, 64), :]], axis=1))
    for par, out in ((0, ge), (1, go)):
        u = jnp.concatenate(us[par], axis=0)
        whole = dot(grad_ref[par], jnp.concatenate([u, u], axis=0))
        out[...] = whole[:, :384]
        g0_ref[par] = whole[:, 384:]

    up_x, up_y = lax.axis_index("gx") % 2 == 0, lax.axis_index("gy") % 2 == 0
    rows = [send_ref[0, 0, k : k + 1, :] for k in range(4)]
    picks = [
        jnp.where(up_y, rows[2], rows[3]),
        jnp.where(up_y, rows[3], rows[2]),
        jnp.where(up_x, rows[0], rows[1]),
        jnp.where(up_x, rows[1], rows[0]),
    ]
    targets = [jnp.broadcast_to(p, (8, 128)) for p in picks]
    outs = (s0_ref, s1_ref, s2_ref, s3_ref)
    for target, out in zip(targets, outs):
        for r in range(0, 384, 8):
            out[pl.ds(r, 8), :] = lane_pick(lambda f: own_ref[pl.ds(r, 8), pl.ds(f * 128, 128)], 6, target)

    total = jnp.zeros((8, 128), F32)
    for q in range(4):

        def points(m, acc, q=q):
            r0 = pl.multiple_of(m * 8, 8)
            w = wjk_ref[pl.ds(r0, 8), :] * weights[q]
            for at, e in zip((q, 7 - q), point_pair(ge, go, q, r0, 8)):
                inv = lax.rsqrt(2.0 * contract(e, e) + DELTA * DELTA)
                wmu = w + (2.0 * w) * inv
                acc = acc + wmu
                here = pl.multiple_of(at * 64 + r0, 8)
                for s in range(6):
                    eu_ref[pl.ds(s * 512 + here, 8), :] = e[s]
                ab_ref[pl.ds(here, 8), :] = 2.0 * wmu
                ab_ref[pl.ds(512 + here, 8), :] = (8.0 * w) * (inv * inv * inv)
            return acc

        total = lax.fori_loop(0, 8, points, total, unroll=4)
    visc = jnp.sum(total, axis=0, keepdims=True) * (1.0 / wsum)
    row = lax.broadcasted_iota(jnp.int32, (8, 128), 0)
    extra = jnp.where(row == 0, visc, jnp.where(row == 1, order.astype(F32), 0.0))
    extra_ref[...] = extra
    for target, out in zip(targets, outs):
        low = jnp.take_along_axis(extra, target & 127, axis=1)
        out[pl.ds(384, 8), :] = jnp.where(target < 768, low, 0.0)


def volume_kernel(
    vhi_ref, vlo_ref, eu_ref, ab_ref, grad_ref, g0_ref, div_hbm, own_ref, extra_ref, links_ref,
    vol_ref, far_ref, hot_ref, pick_ref,
    div_ref, ge, go, sp, sem,
):
    load = pltpu.make_async_copy(div_hbm, div_ref, sem)
    load.start()

    def far(f):
        target = jnp.broadcast_to(links_ref[f], (8, 128))
        lanes = pl.ds(f * 128, 128)
        for r in range(0, 384, 8):
            far_ref[pl.ds(r, 8), lanes] = lane_pick(
                lambda t: own_ref[pl.ds(r, 8), pl.ds(t * 128, 128)], 6, target
            )
        low = jnp.take_along_axis(extra_ref[...], target & 127, axis=1)
        far_ref[pl.ds(384, 8), lanes] = jnp.where(target < 768, low, 0.0)
        slot = target - 768
        k = slot >> 7
        block = jnp.where(k < 2, 2 + (k ^ flip_x), (k - 2) ^ flip_y)
        target = jnp.where((slot < 0) | (slot >= 512), -1, block * 128 + (slot & 127))
        pick_ref[f] = target
        row = lax.broadcasted_iota(jnp.int32, (512, 128), 0)
        hot_ref[:, lanes] = jnp.where(row == target[0:1, :], 1.0, 0.0).astype(BF)

    flip_x, flip_y = lax.axis_index("gx") % 2, lax.axis_index("gy") % 2

    def modes(ref, par, comps):
        rows = [
            jnp.concatenate([ref[pl.ds(c * 512 + i * 64, 64), :] for c in comps], axis=1) for i in range(par, 8, 2)
        ]
        return jnp.concatenate(rows, axis=0)

    for par, out in ((0, ge), (1, go)):
        hi, lo = modes(vhi_ref, par, (1, 2)), modes(vlo_ref, par, (1, 2))
        mat = grad_ref[par]
        left = jnp.concatenate([mat[:, :256], mat], axis=1)
        out[:, 128:] = dot(left, jnp.concatenate([hi, lo, hi], axis=0))
        out[:, :128] = g0_ref[par] + dot(mat[:, :256], modes(vlo_ref, par, (0,)))
    for f in range(3):
        far(f)

    for q in range(4):

        def points(m, carry, q=q):
            r0 = pl.multiple_of(m * 16, 16)
            plus, minus = [[] for _ in range(6)], [[] for _ in range(6)]
            for half in range(2):
                rr = r0 + half * 8
                stress = []
                for at, ev in zip((q, 7 - q), point_pair(ge, go, q, rr, 8)):
                    here = pl.multiple_of(at * 64 + rr, 8)
                    eu = [eu_ref[pl.ds(s * 512 + here, 8), :] for s in range(6)]
                    a = ab_ref[pl.ds(here, 8), :]
                    b = ab_ref[pl.ds(512 + here, 8), :] * contract(eu, ev)
                    stress.append([a * ev[s] - b * eu[s] for s in range(6)])
                for s in range(6):
                    plus[s].append(stress[0][s] + stress[1][s])
                    minus[s].append(stress[0][s] - stress[1][s])
            for s in range(6):
                for k, value in enumerate((plus[s], minus[s])):
                    for j, piece in enumerate(split(jnp.concatenate(value, axis=0))):
                        base = ((s * 2 + k) * 2 + j) * 256 + q * 64
                        sp[pl.ds(pl.multiple_of(base + r0, 16), 16), :] = piece
            return carry

        lax.fori_loop(0, 4, points, 0, unroll=2)

    load.wait()

    def stress(par, j, comps):
        rows = []
        for d in range(3):
            k = (1 if d == 0 else 0) ^ par
            cols = [sp[pl.ds(((SYM[d][c] * 2 + k) * 2 + j) * 256, 256), :] for c in comps]
            rows.append(jnp.concatenate(cols, axis=1))
        return jnp.concatenate(rows, axis=0)

    for par in range(2):
        mat = div_ref[par]
        hi, lo = stress(par, 0, (0, 1)), stress(par, 1, (0, 1))
        left = jnp.concatenate([mat[:, :768], mat], axis=1)
        pair = dot(left, jnp.concatenate([hi, lo, hi], axis=0))
        hi, lo = stress(par, 0, (2,)), stress(par, 1, (2,))
        last = dot(mat[:, :768], jnp.concatenate([hi, lo], axis=1))
        last = (last[:, :128] + last[:, 128:]) + dot(mat[:, 768:], hi)
        for ii in range(4):
            for c, out in enumerate((pair[:, :128], pair[:, 128:], last)):
                vol_ref[pl.ds(c * 512 + (2 * ii + par) * 64, 64), :] = out[ii * 64 : ii * 64 + 64]
    for f in range(3, 6):
        far(f)


def face_kernel(
    order_ref, far_ref, hot_ref, pick_ref, r0_ref, r1_ref, r2_ref, r3_ref, own_ref, extra_ref, links_ref, orient_ref,
    vol_ref, zlift_ref, mab_ref,
    out_ref,
    got, acc, zin,
):
    order = order_ref[...]
    blocks = (r0_ref, r1_ref, r2_ref, r3_ref)
    parts = [split(r[pl.ds(0, MXU_ROWS), :]) for r in blocks]
    left = jnp.concatenate([p[0] for p in parts] + [p[1] for p in parts], axis=1)
    hot = hot_ref[...]
    top = pl.ds(0, MXU_ROWS)
    got[top, :] = far_ref[top, :] + dot(left, jnp.concatenate([hot, hot], axis=0))
    for f in range(6):
        target = pick_ref[f]
        lanes = pl.ds(f * 128, 128)
        for r in range(MXU_ROWS, 392, 8):
            at = (pl.ds(r, 8), lanes)
            got[at] = far_ref[at] + lane_pick(lambda t: blocks[t][pl.ds(r, 8), :], 4, target)

    visc = extra_ref[0:1, :]
    odd_b = lax.broadcasted_iota(jnp.int32, (8, 128), 0) % 2 == 1
    orderf = order.astype(F32)
    face = []
    for f in range(6):
        lanes = pl.ds(f * 128, 128)
        bits = orient_ref[f]
        first = jnp.where(bits % 2 == 1, -1.0, 1.0)
        second = jnp.where(odd_b & (bits >= 2), -1.0, 1.0)
        spin = (second, second * first)
        far_visc, far_order = got[pl.ds(384, 1), lanes], got[pl.ds(385, 1), lanes]
        share = jnp.where(links_ref[f] == 1280, 1.0, 0.5)
        top = jnp.maximum(orderf, far_order) + 1.0
        penalty = 2.0 * top * top * jnp.maximum(visc, far_visc)
        face.append((lanes, spin, share, penalty, share * visc, share * far_visc))

    def flux(f, c, a):
        lanes, spin, share, penalty, weak, weak_far = face[f]
        row, row_h = pl.ds(c * 64 + a * 8, 8), pl.ds(192 + c * 64 + a * 8, 8)
        rot = spin[a % 2]
        mm = mab_ref[pl.ds(a * 8, 8), :]
        jump = own_ref[row, lanes] - rot * got[row, lanes]
        value = mm * (penalty * jump - (weak * own_ref[row_h, lanes] - weak_far * (rot * got[row_h, lanes])))
        return value, mm * (-weak * jump)

    def pair(d, c, a):
        v0, g0 = flux(2 * d, c, a)
        v1, g1 = flux(2 * d + 1, c, a)
        return v1 + v0, v1 - v0, g1 + g0, g1 - g0

    for c in range(3):
        for a in range(8):
            parts = pair(2, c, a)
            for k in range(4):
                zin[pl.ds(k * 64 + a * 8, 8), pl.ds(c * 128, 128)] = parts[k]
    hi, lo = split(zin[...])
    lift = dot(zlift_ref[...], jnp.concatenate([hi, lo], axis=1))
    acc[...] = lift[:, :384] + lift[:, 384:]

    lev = level()
    for c in range(3):
        lanes = pl.ds(c * 128, 128)
        for a in range(8):
            ve, vo, ge, go = pair(1, c, a)
            for j in range(8):
                at = pl.ds(a * 64 + j * 8, 8)
                acc[at, lanes] = acc[at, lanes] + ((vo + SLOPE[j] * go) if j % 2 else (ve + SLOPE[j] * ge))
        for a in range(8):
            ve, vo, ge, go = pair(0, c, a)
            for i in range(8):
                at = pl.ds(i * 64 + a * 8, 8)
                to = pl.ds(c * 512 + i * 64 + a * 8, 8)
                value = acc[at, lanes] + ((vo + SLOPE[i] * go) if i % 2 else (ve + SLOPE[i] * ge))
                live = alive(lev[a * 8 : a * 8 + 8], i, order)
                out_ref[to, :] = jnp.where(live, vol_ref[to, :] + value, 0.0)


def shape(rows, cols=128, kind=F32):
    return jax.ShapeDtypeStruct((rows, cols), kind)


VM = pl.BlockSpec(memory_space=pltpu.VMEM)
HBM = pl.BlockSpec(memory_space=pltpu.HBM)
PARAMS = pltpu.CompilerParams(vmem_limit_bytes=20 * 1024 * 1024)


def partner(s, count, first):
    t = s + 1 if (s - first) % 2 == 0 else s - 1
    return t if first <= min(s, t) and max(s, t) < count else None


def exchange(value, axis, first):
    gx, gy = lax.axis_size("gx"), lax.axis_size("gy")
    links = []
    for x in range(gx):
        for y in range(gy):
            if axis == "gx":
                tx, ty = partner(x, gx, first), y
                if tx is None:
                    tx, ty = x, partner(y, gy, 0)
                    ty = y if ty is None else ty
            else:
                tx, ty = x, partner(y, gy, first)
                if ty is None:
                    ty = gy - 1 - y if gy % 2 == 0 else y
            links.append((x * gy + y, tx * gy + ty))
    return lax.ppermute(value, ("gx", "gy"), links)


def in_hbm(x):
    return pltpu.with_memory_space_constraint(x, pltpu.HBM)


def body(orders, velocity, adjoint_field, face_links, orient, send_faces):
    tab = tables()
    order = orders[0]
    u = velocity.reshape(1536, 128)
    v = adjoint_field.reshape(1536, 128)
    grad, div = jnp.asarray(tab["grad"]), jnp.asarray(tab["div"])
    links, turns = face_links.reshape(6, 1, 128), orient.reshape(6, 1, 128)
    eu, ab, own, extra, vhi, vlo, grad, g0, *packets = pl.pallas_call(
        functools.partial(first_kernel, tab["w"], tab["wsum"]),
        out_shape=[shape(3072), shape(1024), shape(384, 768), shape(8)]
        + [shape(1536, 128, BF)] * 2
        + [jax.ShapeDtypeStruct((2, 768, 512), BF), jax.ShapeDtypeStruct((2, 768, 128), F32)]
        + [shape(392)] * 4,
        in_specs=[HBM] * 7,
        out_specs=[VM] * 12,
        scratch_shapes=[
            pltpu.VMEM((1, 128), jnp.int32),
            pltpu.VMEM((1536, 128), BF),
            pltpu.VMEM((1536, 128), F32),
            pltpu.VMEM((1, 1, 4, 128), jnp.int32),
            pltpu.VMEM((256, 512), BF),
            pltpu.VMEM((64, 128), F32),
            pltpu.VMEM((768, 384), F32),
            pltpu.VMEM((768, 384), F32),
            pltpu.SemaphoreType.DMA((7,)),
        ],
        compiler_params=PARAMS,
        name="state_and_traces",
    )(*map(in_hbm, (order, u, v, send_faces, grad, jnp.asarray(tab["ztrace"]), jnp.asarray(tab["wjk"]))))
    got = [
        exchange(packets[0], "gy", 0),
        exchange(packets[1], "gy", 1),
        exchange(packets[2], "gx", 0),
        exchange(packets[3], "gx", 1),
    ]
    vol, far, hot, pick = pl.pallas_call(
        volume_kernel,
        out_shape=[
            shape(1536),
            shape(392, 768),
            shape(512, 768, BF),
            jax.ShapeDtypeStruct((6, 8, 128), jnp.int32),
        ],
        in_specs=[VM] * 6 + [HBM] + [VM] * 3,
        out_specs=[VM] * 4,
        scratch_shapes=[pltpu.VMEM((2, 256, 1536), BF), pltpu.VMEM((768, 384), F32), pltpu.VMEM((768, 384), F32), pltpu.VMEM((6144, 128), BF), pltpu.SemaphoreType.DMA],
        compiler_params=PARAMS,
        name="volume",
    )(vhi, vlo, eu, ab, grad, g0, in_hbm(div), own, extra, links)
    out = pl.pallas_call(
        face_kernel,
        out_shape=shape(1536),
        in_specs=[VM] * 15,
        out_specs=VM,
        scratch_shapes=[pltpu.VMEM((392, 768), F32), pltpu.VMEM((512, 384), F32), pltpu.VMEM((256, 384), F32)],
        compiler_params=PARAMS,
        name="faces",
    )(
        order, far, hot, pick, *got, own, extra, links, turns, vol,
        jnp.asarray(tab["zlift"]), jnp.asarray(tab["mab"]),
    )
    return out.reshape(1, 1, 3, 512, 128)


def solution(mesh):
    return jax.shard_map(
        body,
        mesh=mesh,
        in_specs=(
            P("gx", "gy", None),
            P("gx", "gy", None, None, None),
            P("gx", "gy", None, None, None),
            P("gx", "gy", None, None),
            P("gx", "gy", None, None),
            P("gx", "gy", None, None),
        ),
        out_specs=P("gx", "gy", None, None, None),
        check_vma=False,
    )
```

```python
import functools

import jax
import jax.numpy as jnp
import numpy as np
from jax import lax
from jax.experimental import pallas as pl
from jax.experimental.pallas import tpu as pltpu
from jax.sharding import PartitionSpec as P

DELTA = 0.05
BF = jnp.bfloat16
F32 = jnp.float32
MXU_ROWS = 256
SLOPE = [i * (i + 1) / 2.0 for i in range(8)]
MASS = [2.0 / (2.0 * i + 1.0) for i in range(8)]
SYM = [[0, 3, 4], [3, 1, 5], [4, 5, 2]]


def split_np(x):
    hi = np.asarray(x, np.float32).astype(BF)
    lo = np.asarray(x - hi.astype(np.float64), np.float32).astype(BF)
    return hi, lo


@functools.cache
def tables():
    q = np.arange(8)
    x = np.cos(np.pi * (q + 0.5) / 8.0)
    w = np.pi / 8.0 * np.sqrt(1.0 - x * x)
    values, slopes = [np.ones(8), x], [np.zeros(8), np.ones(8)]
    for k in range(1, 7):
        values.append(((2 * k + 1) * x * values[k] - k * values[k - 1]) / (k + 1))
        slopes.append(slopes[k - 1] + (2 * k + 1) * values[k])
    leg, der = np.stack(values, 1), np.stack(slopes, 1)
    grads, divs = [], []
    for par in range(2):
        li, di = leg[:4, par::2], der[:4, par::2]
        full = np.concatenate(
            [
                np.kron(di, np.kron(leg, leg)),
                np.kron(li, np.kron(der, leg)),
                np.kron(li, np.kron(leg, der)),
            ],
            axis=0,
        )
        grads.append(np.concatenate(split_np(full), axis=1))
        divs.append(np.concatenate(split_np(full.T), axis=1))
    sign = (-1.0) ** q
    slope = np.array(SLOPE)
    eye = np.eye(64)
    ztrace = np.concatenate([np.kron(eye, v[None]) for v in (sign, np.ones(8), sign * slope, slope)], 0)
    even = (q % 2 == 0).astype(np.float64)
    odd = 1.0 - even
    zlift = np.concatenate([np.kron(eye, v[:, None]) for v in (even, odd, even * slope, odd * slope)], 1)
    wjk = np.broadcast_to(np.kron(w, w)[:, None], (64, 128))
    mass = np.array(MASS)
    mab = np.broadcast_to(np.kron(mass, mass)[:, None], (64, 128))
    return dict(
        grad=np.stack(grads),
        div=np.stack(divs),
        ztrace=ztrace.astype(BF),
        zlift=zlift.astype(BF),
        wjk=np.asarray(wjk, np.float32),
        mab=np.asarray(mab, np.float32),
        w=[float(v) for v in w],
        wsum=float(np.sum(w) ** 3),
    )


def dot(a, b):
    return jnp.dot(a, b, preferred_element_type=F32)


def split(x):
    hi = x.astype(BF)
    return hi, (x - hi.astype(F32)).astype(BF)


def level():
    row = lax.broadcasted_iota(jnp.int32, (64, 128), 0)
    return jnp.maximum(row // 8, row % 8)


def alive(lev, i, order):
    return jnp.maximum(lev, i) <= order


def lane_pick(get, count, target):
    low, tile = target & 127, target >> 7
    out = jnp.zeros(target.shape, F32)
    for t in range(count):
        out = jnp.where(tile == t, jnp.take_along_axis(get(t), low, axis=1), out)
    return out


def aligned(x):
    return x if isinstance(x, int) else pl.multiple_of(x, 8)


def point_pair(ge, go, q, r0, rows):
    even, odd = {}, {}
    for d in range(3):
        for c in range(3):
            at = (pl.ds(aligned(d * 256 + q * 64 + r0), rows), pl.ds(c * 128, 128))
            even[d, c], odd[d, c] = ge[at], go[at]

    def strain(g):
        return [
            g[0, 0], g[1, 1], g[2, 2],
            0.5 * (g[0, 1] + g[1, 0]), 0.5 * (g[0, 2] + g[2, 0]), 0.5 * (g[1, 2] + g[2, 1]),
        ]

    near = {k: even[k] + odd[k] for k in even}
    far = {k: odd[k] - even[k] if k[0] == 0 else even[k] - odd[k] for k in even}
    return strain(near), strain(far)


def contract(a, b):
    return (a[0] * b[0] + a[1] * b[1] + a[2] * b[2]) + 2.0 * (a[3] * b[3] + a[4] * b[4] + a[5] * b[5])


def first_kernel(
    weights, wsum,
    order_hbm, u_hbm, v_hbm, send_hbm, grad_hbm, ztrace_hbm, wjk_hbm,
    eu_ref, ab_ref, own_ref, extra_ref, vhi_ref, vlo_ref, grad_ref, g0_ref, s0_ref, s1_ref, s2_ref, s3_ref,
    order_ref, u_ref, v_ref, send_ref, ztrace_ref, wjk_ref, ge, go, sems,
):
    names = ("order", "v", "ztrace", "send", "u", "wjk", "grad0", "grad1")
    ends = (
        (order_hbm, order_ref), (v_hbm, v_ref), (ztrace_hbm, ztrace_ref), (send_hbm, send_ref), (u_hbm, u_ref),
        (wjk_hbm, wjk_ref), (grad_hbm.at[0], grad_ref.at[0]), (grad_hbm.at[1], grad_ref.at[1]),
    )
    loads = {n: pltpu.make_async_copy(*e, sems.at[k]) for k, (n, e) in enumerate(zip(names, ends))}
    for n in names:
        loads[n].start()
    loads["order"].wait()
    order = order_ref[...]
    lev = level()
    loads["v"].wait()
    for i in range(8):
        live = alive(lev, i, order)
        for c in range(3):
            at = pl.ds(c * 512 + i * 64, 64)
            value = jnp.where(live, v_ref[at, :], 0.0)
            v_ref[at, :] = value
            vhi_ref[at, :], vlo_ref[at, :] = split(value)

    def put(c, row, rows, d, even_v, odd_v, even_g, odd_g):
        for s in range(2):
            lanes = pl.ds((2 * d + s) * 128, 128)
            own_ref[pl.ds(c * 64 + row, rows), lanes] = even_v + odd_v if s else even_v - odd_v
            own_ref[pl.ds(192 + c * 64 + row, rows), lanes] = even_g + odd_g if s else even_g - odd_g

    def sums(get):
        v = [get(i) for i in range(8)]
        return (
            (v[0] + v[2]) + (v[4] + v[6]),
            (v[1] + v[3]) + (v[5] + v[7]),
            (3.0 * v[2] + 10.0 * v[4]) + 21.0 * v[6],
            (v[1] + 6.0 * v[3]) + (15.0 * v[5] + 28.0 * v[7]),
        )

    for c in range(3):
        for m in range(8):
            put(c, m * 8, 8, 0, *sums(lambda i: v_ref[pl.ds(c * 512 + i * 64 + m * 8, 8), :]))
        for i in range(8):
            put(c, i * 8, 8, 1, *sums(lambda j: v_ref[pl.ds(c * 512 + i * 64 + j * 8, 8), :]))
    loads["ztrace"].wait()
    loads["send"].wait()
    both = jnp.concatenate([r[pl.ds(c * 512, 512), :] for r in (vhi_ref, vlo_ref) for c in range(3)], axis=1)
    z = dot(ztrace_ref[...], both)
    for c in range(3):
        block = z[:, c * 128 : (c + 1) * 128] + z[:, 384 + c * 128 : 512 + c * 128]
        for s in range(2):
            lanes = pl.ds((4 + s) * 128, 128)
            own_ref[pl.ds(c * 64, 64), lanes] = block[s * 64 : (s + 1) * 64]
            own_ref[pl.ds(192 + c * 64, 64), lanes] = block[128 + s * 64 : 192 + s * 64]

    up_x, up_y = lax.axis_index("gx") % 2 == 0, lax.axis_index("gy") % 2 == 0
    rows = [send_ref[0, 0, k : k + 1, :] for k in range(4)]
    picks = [
        jnp.where(up_y, rows[2], rows[3]),
        jnp.where(up_y, rows[3], rows[2]),
        jnp.where(up_x, rows[0], rows[1]),
        jnp.where(up_x, rows[1], rows[0]),
    ]
    targets = [jnp.broadcast_to(p, (8, 128)) for p in picks]
    outs = (s0_ref, s1_ref, s2_ref, s3_ref)

    def pack(k):
        for r in range(0, 384, 8):
            outs[k][pl.ds(r, 8), :] = lane_pick(
                lambda f: own_ref[pl.ds(r, 8), pl.ds(f * 128, 128)], 6, targets[k]
            )

    pack(0)
    for n in ("u", "wjk", "grad0", "grad1"):
        loads[n].wait()
    us = [[], []]
    for i in range(8):
        live = alive(lev, i, order)
        row = [
            jnp.where(live, u_ref[pl.ds(c * 512 + i * 64, 64), :].astype(F32), 0.0).astype(BF)
            for c in range(3)
        ]
        us[i % 2].append(jnp.concatenate(row + [vhi_ref[pl.ds(i * 64, 64), :]], axis=1))
    pack(1)
    for par, out in ((0, ge), (1, go)):
        u = jnp.concatenate(us[par], axis=0)
        whole = dot(grad_ref[par], jnp.concatenate([u, u], axis=0))
        out[...] = whole[:, :384]
        g0_ref[par] = whole[:, 384:]
    pack(2)
    pack(3)

    total = jnp.zeros((8, 128), F32)
    for q in range(4):

        def points(m, acc, q=q):
            r0 = m * 8
            w = wjk_ref[pl.ds(r0, 8), :] * weights[q]
            for at, e in zip((q, 7 - q), point_pair(ge, go, q, r0, 8)):
                inv = lax.rsqrt(2.0 * contract(e, e) + DELTA * DELTA)
                wmu = w + (2.0 * w) * inv
                acc = acc + wmu
                here = at * 64 + r0
                for s in range(6):
                    eu_ref[pl.ds(s * 512 + here, 8), :] = e[s]
                ab_ref[pl.ds(here, 8), :] = 2.0 * wmu
                ab_ref[pl.ds(512 + here, 8), :] = (8.0 * w) * (inv * inv * inv)
            return acc

        for m in range(8):
            total = points(m, total)
    visc = jnp.sum(total, axis=0, keepdims=True) * (1.0 / wsum)
    row = lax.broadcasted_iota(jnp.int32, (8, 128), 0)
    extra = jnp.where(row == 0, visc, jnp.where(row == 1, order.astype(F32), 0.0))
    extra_ref[...] = extra
    for target, out in zip(targets, outs):
        low = jnp.take_along_axis(extra, target & 127, axis=1)
        out[pl.ds(384, 8), :] = jnp.where(target < 768, low, 0.0)


def face_signs(bits):
    odd_b = lax.broadcasted_iota(jnp.int32, (8, 128), 0) % 2 == 1
    second = jnp.where(odd_b & (bits >= 2), -1.0, 1.0)
    return second, second * jnp.where(bits % 2 == 1, -1.0, 1.0)


def volume_kernel(
    vhi_ref, vlo_ref, eu_ref, ab_ref, grad_ref, g0_ref, div_hbm, own_ref, extra_ref, links_ref, orient_ref, mab_ref,
    vol_ref, jump_ref, part_ref, aux_ref, hot_ref, pick_ref,
    div_ref, ge, go, sp, sem,
):
    load = pltpu.make_async_copy(div_hbm, div_ref, sem)
    load.start()

    def far(f):
        target = jnp.broadcast_to(links_ref[f], (8, 128))
        lanes = pl.ds(f * 128, 128)
        aux = jnp.where(target < 768, jnp.take_along_axis(extra_ref[...], target & 127, axis=1), 0.0)
        aux_ref[f] = aux
        spin = face_signs(orient_ref[f])
        share = jnp.where(links_ref[f] == 1280, 1.0, 0.5)
        weak, weak_far = share * extra_ref[0:1, :], share * aux[0:1, :]
        for a in range(8):
            mm = mab_ref[pl.ds(a * 8, 8), :]
            own_part, far_part = mm * weak, mm * weak_far * spin[a % 2]
            for c in range(3):
                at, at_g = pl.ds(c * 64 + a * 8, 8), pl.ds(192 + c * 64 + a * 8, 8)
                far_t = lane_pick(lambda t: own_ref[at, pl.ds(t * 128, 128)], 6, target)
                far_g = lane_pick(lambda t: own_ref[at_g, pl.ds(t * 128, 128)], 6, target)
                jump_ref[at, lanes] = own_ref[at, lanes] - spin[a % 2] * far_t
                part_ref[at, lanes] = far_part * far_g - own_part * own_ref[at_g, lanes]
        slot = target - 768
        k = slot >> 7
        block = jnp.where(k < 2, 2 + (k ^ flip_x), (k - 2) ^ flip_y)
        target = jnp.where((slot < 0) | (slot >= 512), -1, block * 128 + (slot & 127))
        pick_ref[f] = target
        row = lax.broadcasted_iota(jnp.int32, (512, 128), 0)
        hot_ref[:, lanes] = jnp.where(row == target[0:1, :], 1.0, 0.0).astype(BF)

    flip_x, flip_y = lax.axis_index("gx") % 2, lax.axis_index("gy") % 2

    def modes(ref, par, comps):
        rows = [
            jnp.concatenate([ref[pl.ds(c * 512 + i * 64, 64), :] for c in comps], axis=1) for i in range(par, 8, 2)
        ]
        return jnp.concatenate(rows, axis=0)

    for par, out in ((0, ge), (1, go)):
        hi, lo = modes(vhi_ref, par, (1, 2)), modes(vlo_ref, par, (1, 2))
        mat = grad_ref[par]
        left = jnp.concatenate([mat[:, :256], mat], axis=1)
        out[:, 128:] = dot(left, jnp.concatenate([hi, lo, hi], axis=0))
        out[:, :128] = g0_ref[par] + dot(mat[:, :256], modes(vlo_ref, par, (0,)))
    for f in range(3):
        far(f)

    for q in range(4):

        def points(m, carry, q=q):
            r0 = pl.multiple_of(m * 16, 16)
            plus, minus = [[] for _ in range(6)], [[] for _ in range(6)]
            for half in range(2):
                rr = r0 + half * 8
                stress = []
                for at, ev in zip((q, 7 - q), point_pair(ge, go, q, rr, 8)):
                    here = pl.multiple_of(at * 64 + rr, 8)
                    eu = [eu_ref[pl.ds(s * 512 + here, 8), :] for s in range(6)]
                    a = ab_ref[pl.ds(here, 8), :]
                    b = ab_ref[pl.ds(512 + here, 8), :] * contract(eu, ev)
                    stress.append([a * ev[s] - b * eu[s] for s in range(6)])
                for s in range(6):
                    plus[s].append(stress[0][s] + stress[1][s])
                    minus[s].append(stress[0][s] - stress[1][s])
            for s in range(6):
                for k, value in enumerate((plus[s], minus[s])):
                    for j, piece in enumerate(split(jnp.concatenate(value, axis=0))):
                        base = ((s * 2 + k) * 2 + j) * 256 + q * 64
                        sp[pl.ds(pl.multiple_of(base + r0, 16), 16), :] = piece
            return carry

        lax.fori_loop(0, 4, points, 0, unroll=2)

    load.wait()

    def stress(par, j, comps):
        rows = []
        for d in range(3):
            k = (1 if d == 0 else 0) ^ par
            cols = [sp[pl.ds(((SYM[d][c] * 2 + k) * 2 + j) * 256, 256), :] for c in comps]
            rows.append(jnp.concatenate(cols, axis=1))
        return jnp.concatenate(rows, axis=0)

    for par in range(2):
        mat = div_ref[par]
        hi, lo = stress(par, 0, (0, 1)), stress(par, 1, (0, 1))
        left = jnp.concatenate([mat[:, :768], mat], axis=1)
        pair = dot(left, jnp.concatenate([hi, lo, hi], axis=0))
        hi, lo = stress(par, 0, (2,)), stress(par, 1, (2,))
        last = dot(mat[:, :768], jnp.concatenate([hi, lo], axis=1))
        last = (last[:, :128] + last[:, 128:]) + dot(mat[:, 768:], hi)
        for ii in range(4):
            for c, out in enumerate((pair[:, :128], pair[:, 128:], last)):
                vol_ref[pl.ds(c * 512 + (2 * ii + par) * 64, 64), :] = out[ii * 64 : ii * 64 + 64]
    for f in range(3, 6):
        far(f)


def face_kernel(
    order_ref, jump_ref, part_ref, aux_ref, hot_ref, pick_ref, r0_ref, r1_ref, r2_ref, r3_ref, extra_ref,
    links_ref, orient_ref, vol_ref, zlift_ref, mab_ref,
    out_ref,
    got, acc, zin,
):
    order = order_ref[...]
    blocks = (r0_ref, r1_ref, r2_ref, r3_ref)
    parts = [split(r[pl.ds(0, MXU_ROWS), :]) for r in blocks]
    left = jnp.concatenate([p[0] for p in parts] + [p[1] for p in parts], axis=1)
    hot = hot_ref[...]
    got[pl.ds(0, MXU_ROWS), :] = dot(left, jnp.concatenate([hot, hot], axis=0))
    for f in range(6):
        for r in range(MXU_ROWS, 392, 8):
            got[pl.ds(r, 8), pl.ds(f * 128, 128)] = lane_pick(
                lambda t: blocks[t][pl.ds(r, 8), :], 4, pick_ref[f]
            )

    visc = extra_ref[0:1, :]
    orderf = order.astype(F32)
    face = []
    for f in range(6):
        lanes = pl.ds(f * 128, 128)
        spin = face_signs(orient_ref[f])
        recv_visc, recv_order = got[pl.ds(384, 1), lanes], got[pl.ds(385, 1), lanes]
        share = jnp.where(links_ref[f] == 1280, 1.0, 0.5)
        top = jnp.maximum(orderf, aux_ref[f, 1:2, :] + recv_order) + 1.0
        penalty = 2.0 * top * top * jnp.maximum(visc, aux_ref[f, 0:1, :] + recv_visc)
        face.append((lanes, spin, penalty, share * visc, share * recv_visc))

    def flux(f, c, a):
        lanes, spin, penalty, weak, weak_far = face[f]
        row, row_g = pl.ds(c * 64 + a * 8, 8), pl.ds(192 + c * 64 + a * 8, 8)
        mm = mab_ref[pl.ds(a * 8, 8), :]
        jump = jump_ref[row, lanes] - spin[a % 2] * got[row, lanes]
        value = (mm * penalty) * jump + (part_ref[row, lanes] + (mm * weak_far * spin[a % 2]) * got[row_g, lanes])
        return value, (mm * -weak) * jump

    def pair(d, c, a):
        v0, g0 = flux(2 * d, c, a)
        v1, g1 = flux(2 * d + 1, c, a)
        return v1 + v0, v1 - v0, g1 + g0, g1 - g0

    for a in range(8):
        for c in range(3):
            parts = pair(2, c, a)
            for k in range(4):
                zin[pl.ds(k * 64 + a * 8, 8), pl.ds(c * 128, 128)] = parts[k]
    hi, lo = split(zin[...])
    lift = dot(zlift_ref[...], jnp.concatenate([hi, lo], axis=1))
    acc[...] = lift[:, :384] + lift[:, 384:]

    lev = level()
    for a in range(8):
        for c in range(3):
            lanes = pl.ds(c * 128, 128)
            ve, vo, ge, go = pair(1, c, a)
            for j in range(8):
                at = pl.ds(a * 64 + j * 8, 8)
                acc[at, lanes] = acc[at, lanes] + ((vo + SLOPE[j] * go) if j % 2 else (ve + SLOPE[j] * ge))
    for a in range(8):
        live = [alive(lev[a * 8 : a * 8 + 8], i, order) for i in range(8)]
        for c in range(3):
            lanes = pl.ds(c * 128, 128)
            ve, vo, ge, go = pair(0, c, a)
            for i in range(8):
                at = pl.ds(i * 64 + a * 8, 8)
                to = pl.ds(c * 512 + i * 64 + a * 8, 8)
                value = acc[at, lanes] + ((vo + SLOPE[i] * go) if i % 2 else (ve + SLOPE[i] * ge))
                out_ref[to, :] = jnp.where(live[i], vol_ref[to, :] + value, 0.0)


def shape(rows, cols=128, kind=F32):
    return jax.ShapeDtypeStruct((rows, cols), kind)


VM = pl.BlockSpec(memory_space=pltpu.VMEM)
HBM = pl.BlockSpec(memory_space=pltpu.HBM)
PARAMS = pltpu.CompilerParams(vmem_limit_bytes=20 * 1024 * 1024)


def partner(s, count, first):
    t = s + 1 if (s - first) % 2 == 0 else s - 1
    return t if first <= min(s, t) and max(s, t) < count else None


def exchange(value, axis, first):
    gx, gy = lax.axis_size("gx"), lax.axis_size("gy")
    links = []
    for x in range(gx):
        for y in range(gy):
            if axis == "gx":
                tx, ty = partner(x, gx, first), y
                if tx is None:
                    tx, ty = x, partner(y, gy, 0)
                    ty = y if ty is None else ty
            else:
                tx, ty = x, partner(y, gy, first)
                if ty is None:
                    ty = gy - 1 - y if gy % 2 == 0 else y
            links.append((x * gy + y, tx * gy + ty))
    return lax.ppermute(value, ("gx", "gy"), links)


def in_hbm(x):
    return pltpu.with_memory_space_constraint(x, pltpu.HBM)


def body(orders, velocity, adjoint_field, face_links, orient, send_faces):
    tab = tables()
    order = orders[0]
    u = velocity.reshape(1536, 128)
    v = adjoint_field.reshape(1536, 128)
    mab = jnp.asarray(tab["mab"])
    grad, div = jnp.asarray(tab["grad"]), jnp.asarray(tab["div"])
    links, turns = face_links.reshape(6, 1, 128), orient.reshape(6, 1, 128)
    eu, ab, own, extra, vhi, vlo, grad, g0, *packets = pl.pallas_call(
        functools.partial(first_kernel, tab["w"], tab["wsum"]),
        out_shape=[shape(3072), shape(1024), shape(384, 768), shape(8)]
        + [shape(1536, 128, BF)] * 2
        + [jax.ShapeDtypeStruct((2, 768, 512), BF), jax.ShapeDtypeStruct((2, 768, 128), F32)]
        + [shape(392)] * 4,
        in_specs=[HBM] * 7,
        out_specs=[VM] * 12,
        scratch_shapes=[
            pltpu.VMEM((1, 128), jnp.int32),
            pltpu.VMEM((1536, 128), BF),
            pltpu.VMEM((1536, 128), F32),
            pltpu.VMEM((1, 1, 4, 128), jnp.int32),
            pltpu.VMEM((256, 512), BF),
            pltpu.VMEM((64, 128), F32),
            pltpu.VMEM((768, 384), F32),
            pltpu.VMEM((768, 384), F32),
            pltpu.SemaphoreType.DMA((8,)),
        ],
        compiler_params=PARAMS,
        name="state_and_traces",
    )(*map(in_hbm, (order, u, v, send_faces, grad, jnp.asarray(tab["ztrace"]), jnp.asarray(tab["wjk"]))))
    got = [
        exchange(packets[0], "gy", 0),
        exchange(packets[1], "gy", 1),
        exchange(packets[2], "gx", 0),
        exchange(packets[3], "gx", 1),
    ]
    vol, jump, part, aux, hot, pick = pl.pallas_call(
        volume_kernel,
        out_shape=[
            shape(1536),
            shape(192, 768),
            shape(192, 768),
            jax.ShapeDtypeStruct((6, 8, 128), F32),
            shape(512, 768, BF),
            jax.ShapeDtypeStruct((6, 8, 128), jnp.int32),
        ],
        in_specs=[VM] * 6 + [HBM] + [VM] * 5,
        out_specs=[VM] * 6,
        scratch_shapes=[pltpu.VMEM((2, 256, 1536), BF), pltpu.VMEM((768, 384), F32), pltpu.VMEM((768, 384), F32), pltpu.VMEM((6144, 128), BF), pltpu.SemaphoreType.DMA],
        compiler_params=PARAMS,
        name="volume",
    )(vhi, vlo, eu, ab, grad, g0, in_hbm(div), own, extra, links, turns, mab)
    out = pl.pallas_call(
        face_kernel,
        out_shape=shape(1536),
        in_specs=[VM] * 16,
        out_specs=VM,
        scratch_shapes=[
            pltpu.VMEM((392, 768), F32),
            pltpu.VMEM((512, 384), F32),
            pltpu.VMEM((256, 384), F32),
        ],
        compiler_params=PARAMS,
        name="faces",
    )(
        order, jump, part, aux, hot, pick, *got, extra, links, turns, vol,
        jnp.asarray(tab["zlift"]), mab,
    )
    return out.reshape(1, 1, 3, 512, 128)


def solution(mesh):
    return jax.shard_map(
        body,
        mesh=mesh,
        in_specs=(
            P("gx", "gy", None),
            P("gx", "gy", None, None, None),
            P("gx", "gy", None, None, None),
            P("gx", "gy", None, None),
            P("gx", "gy", None, None),
            P("gx", "gy", None, None),
        ),
        out_specs=P("gx", "gy", None, None, None),
        check_vma=False,
    )
```
